32 devices in a mesh: dp: 16 (over z, x, core), tensor: 2 (over y).
Axes of the slice: x: 2, y: 2, z: 4, core: 2. Of those that a mesh axis runs over, the one named last changes fastest.
Arguments:
- tokens: bfloat16 [16384, 1024], P(('dp', 'tensor')), may hold values from -6 to 6
- cotangent: bfloat16 [16384, 1024], P(('dp', 'tensor')), may hold values from -6 to 6
- lengths: int32 [16, 8], P('dp'), may hold values from 1 to 512, 1024 in all within a row
- ln1_gain: bfloat16 [1024], P('dp'), may hold values from 0.5 to 1.5
- ln1_bias: bfloat16 [1024], P('dp'), may hold values from -3 to 3
- qkv_weight: bfloat16 [1024, 3, 1024], P('dp', None, 'tensor')
- qkv_bias: bfloat16 [2, 16, 64], P(None, 'tensor', 'dp'), may hold values from -3 to 3
- out_weight: bfloat16 [1024, 1024], P('tensor', 'dp'), may hold values from -0.375 to 0.375
- out_bias: bfloat16 [1024], P('dp'), may hold values from -3 to 3
- ln2_gain: bfloat16 [1024], P('dp'), may hold values from 0.5 to 1.5
- ln2_bias: bfloat16 [1024], P('dp'), may hold values from -3 to 3
- up_weight: bfloat16 [1024, 4096], P('dp', 'tensor'), may hold values from -0.1875 to 0.1875
- up_bias: bfloat16 [64, 64], P('tensor', 'dp'), may hold values from -3 to 3
- down_weight: bfloat16 [4096, 1024], P('tensor', 'dp'), may hold values from -0.09375 to 0.09375
- down_bias: bfloat16 [1024], P('dp'), may hold values from -3 to 3
Outputs:
- output: float32 [16384, 1024], P(('dp', 'tensor'))
- grad_tokens: float32 [16384, 1024], P(('dp', 'tensor'))
- grad_ln1_gain: float32 [1024], P('dp')
- grad_ln1_bias: float32 [1024], P('dp')
- grad_qkv_weight: float32 [1024, 3, 1024], P('dp', None, 'tensor')
- grad_qkv_bias: float32 [2, 16, 64], P(None, 'tensor', 'dp')
- grad_out_weight: float32 [1024, 1024], P('tensor', 'dp')
- grad_out_bias: float32 [1024], P('dp')
- grad_ln2_gain: float32 [1024], P('dp')
- grad_ln2_bias: float32 [1024], P('dp')
- grad_up_weight: float32 [1024, 4096], P('dp', 'tensor')
- grad_up_bias: float32 [64, 64], P('tensor', 'dp')
- grad_down_weight: float32 [4096, 1024], P('tensor', 'dp')
- grad_down_bias: float32 [1024], P('dp')
The draws below stay inside these ranges and needn't reach their ends.
Inputs may be any that keep to these rules, and one draw needn't show every extreme that they name: Row g of lengths holds the 8 packed sequences of group g in order; each row sums to 1024 and holds a length of exactly 512.
All inputs are finite; a program needn't handle non-finite values.
Results may differ from the reference program's by a relative error of at most 0.02.
Values may be sent and summed in bfloat16 or wider, within the bound.
No kernel may reach another device: no remote copies, remote signals or barrier semaphores. Data moves between devices by JAX's collectives and lax.ppermute only.
A program may use at most 192 MiB of HBM per device.

```python
import math
import jax
import jax.numpy as jnp
import numpy as np
from jax import lax

D = 1024
H = 16
HD = 64
FF = 4096
ROWS = 1024
LMAX = 512
SEQS = 8
GROUPS = 16
TOKENS = 16384


def draw_qkv_weight(key, part):
    second_key = jax.random.fold_in(jax.random.fold_in(key, 11), 1)
    weight_scale = D ** (-0.5)
    whole = jax.random.normal(second_key, (D, 3, D), jnp.float32) * weight_scale
    return whole.astype(jnp.bfloat16)


def raised(values, key, source, target, blocks, factor):
    def block_of(position):
        return (jnp.arange(values.shape[position]) // (values.shape[position] // blocks)).reshape((-1,) + (1,) * (values.ndim - 1 - position))

    one_side = jax.random.permutation(key, blocks)[block_of(target)]
    second = (block_of(target) + blocks // 2) % blocks
    return jnp.where((block_of(source) == one_side) | (block_of(source) == second), factor * values, values)


def levels(own_key, dims, shards, smallest, high):
    factor_of, own = 1.0, jax.random.fold_in(own_key, 6)
    for axis_at, parts in shards:
        draws = jnp.exp(jax.random.uniform(jax.random.fold_in(own, axis_at), (parts,), jnp.float32, smallest / len(shards), high / len(shards)))
        factor_of = factor_of * jnp.repeat(draws, dims[axis_at] // parts).reshape([-1 if axis == axis_at else 1 for axis in range(len(dims))])
    return factor_of


def split_up(number_of, total, limit, skew):
    weights = [(1 << 20) // math.isqrt(rank ** skew) + 1 for rank in range(2, number_of + 1)]
    rest, holding = total - limit - (number_of - 1), [1] * (number_of - 1)
    while rest > 0:
        free = [i for i in range(number_of - 1) if holding[i] < limit]
        pool, budget = sum([weights[i] for i in free]), rest
        for i in free:
            addition = min(limit - holding[i], max(1, budget * weights[i] // pool), rest)
            holding[i] = holding[i] + addition
            rest = rest - addition
    return np.array([limit] + holding)


def uneven_parts(rng, count, total, bound, skew):
    if count == 2:
        one = jax.random.randint(rng, (), max(1, total - bound), min(bound, total - 1) + 1)
        return jnp.stack([one, total - one])
    sizes = jnp.asarray(split_up(count, total, bound, skew), jnp.int32)
    twos = (count - 1) // 2
    giver, taker = sizes[1:1 + 2 * twos:2], sizes[2:2 + 2 * twos:2]
    room = jnp.minimum(giver - 1, bound - taker)
    moved = jax.random.randint(jax.random.fold_in(rng, 1), (twos,), 0, 1 << 20) % (room + 1)
    sizes = sizes.at[1:1 + 2 * twos:2].set(giver - moved).at[2:2 + 2 * twos:2].set(taker + moved)
    return sizes[jax.random.permutation(jax.random.fold_in(rng, 2), count)]


def centred(rng, dims, spread, most, cuts=(), kind=jnp.bfloat16):
    result = jax.random.normal(rng, dims, jnp.float32) * spread
    if len(cuts) > 0:
        result = levels(rng, dims, cuts, -0.22, 0.18) * result
    return jnp.clip(result, min=-most, max=most).astype(kind)


def noise_with(stream_key, shape, scale, limit, cuts, heavy, kind=jnp.bfloat16):
    values = scale * jax.random.normal(stream_key, shape, jnp.float32)
    if cuts:
        values = values * levels(stream_key, shape, cuts, -0.22, 0.18)
    return jnp.clip(raised(values, jax.random.fold_in(stream_key, 3), *heavy), -limit, limit).astype(kind)


def setup_inputs(seed: int = 0) -> dict:
    key_of = jax.random.split(jax.random.key(seed), 16)
    return {
        "tokens": centred(key_of[0], (TOKENS, D), 1.0, 6.0, ((0, 32),)),
        "cotangent": noise_with(key_of[1], (TOKENS, D), 1.0, 6.0, ((0, 32),), (0, 1, 32, 2.75)),
        "lengths": jax.vmap(lambda own: uneven_parts(own, SEQS, ROWS, LMAX, 2))(jax.random.split(key_of[2], GROUPS)).reshape((GROUPS, SEQS)).astype(jnp.int32),
        "ln1_gain": jnp.clip(1.0 + 0.1 * jax.random.normal(key_of[3], (D,), jnp.float32), 0.5, 1.5).astype(jnp.bfloat16),
        "ln1_bias": centred(key_of[4], (D,), 0.5, 3.0, ((0, 16),)),
        "qkv_weight": draw_qkv_weight(jax.random.fold_in(key_of[15], 71), 0),
        "qkv_bias": centred(key_of[6], (2, H, HD), 0.5, 3.0, ((1, 2), (2, 16))),
        "out_weight": centred(key_of[7], (D, D), (D // 4) ** -0.5, 0.375, ((0, 2), (1, 16))),
        "out_bias": centred(key_of[8], (D,), 0.5, 3.0, ((0, 16),)),
        "ln2_gain": jnp.clip(1.0 + 0.1 * jax.random.normal(key_of[9], (D,), jnp.float32), 0.5, 1.5).astype(jnp.bfloat16),
        "ln2_bias": centred(key_of[10], (D,), 0.5, 3.0, ((0, 16),)),
        "up_weight": centred(key_of[11], (D, FF), D ** -0.5, 0.1875, ((0, 16), (1, 2))),
        "up_bias": centred(key_of[12], (FF // HD, HD), 0.5, 3.0, ((0, 2), (1, 16))),
        "down_weight": centred(key_of[13], (FF, D), FF ** -0.5, 0.09375, ((0, 2), (1, 16))),
        "down_bias": centred(key_of[14], (D,), 0.5, 3.0, ((0, 16),)),
    }


epsilon = 1e-05
gelu_root = math.sqrt(2.0 / math.pi)
gelu_cubic = 0.044715
masked_score = -1e+30

def normalize(values, norm_gain, offset):
    center = values - lax.optimization_barrier(jnp.mean(values, axis=-1, keepdims=True))
    inverse = lax.rsqrt(lax.optimization_barrier(jnp.mean(center * center, axis=-1, keepdims=True)) + epsilon)
    scaled = center * inverse
    return (scaled, inverse, scaled * norm_gain + offset)

def normalize_back(upstream, scaled, inverse, norm_gain):
    weighted = upstream * norm_gain
    return inverse * (weighted - lax.optimization_barrier(jnp.mean(weighted, axis=-1, keepdims=True)) - scaled * lax.optimization_barrier(jnp.mean(weighted * scaled, axis=-1, keepdims=True)))

def gelu_value(values):
    return 0.5 * values * (1.0 + jnp.tanh(gelu_root * (values + gelu_cubic * values * values * values)))

def gelu_slope(values):
    tangent = jnp.tanh(gelu_root * (values + gelu_cubic * values * values * values))
    inner_slope = gelu_root * (1.0 + 3.0 * gelu_cubic * values * values)
    return 0.5 * (1.0 + tangent) + 0.5 * values * (1.0 - tangent * tangent) * inner_slope

def segment_ids(length_row, row_total):
    seq_ends = jnp.cumsum(length_row.astype(jnp.int32))
    places = jnp.arange(row_total, dtype=jnp.int32)
    return lax.optimization_barrier(jnp.sum((places[:, None] >= seq_ends[None, :-1]).astype(jnp.int32), axis=1))

def block_scores(query_rows, key_rows, segments, block_index, block_rows):
    row_total = key_rows.shape[0]
    score_scale = query_rows.shape[2] ** (-0.5)
    places = jnp.arange(row_total, dtype=jnp.int32)
    first_row = (block_index * block_rows).astype(jnp.int32)
    query_block = lax.dynamic_slice_in_dim(query_rows, first_row, block_rows, 0)
    query_segments = lax.dynamic_slice_in_dim(segments, first_row, block_rows, 0)
    query_places = first_row + jnp.arange(block_rows, dtype=jnp.int32)
    allowed = (query_segments[:, None] == segments[None, :]) & (places[None, :] <= query_places[:, None])
    scores = jnp.einsum('qhd,khd->hqk', query_block.astype(jnp.float32), key_rows.astype(jnp.float32)) * score_scale
    return (jnp.where(allowed[None], scores, masked_score), query_block, first_row)

def attention_forward(query_rows, key_rows, value_rows, segments):
    row_total, head_count, head_width = query_rows.shape
    block_rows = min(512, row_total)

    def one_block(block_index):
        scores, query_block, first_row = block_scores(query_rows, key_rows, segments, block_index, block_rows)
        row_peak = lax.optimization_barrier(jnp.max(scores, axis=-1, keepdims=True))
        exponent = jnp.exp(scores - row_peak)
        row_sum = lax.optimization_barrier(jnp.sum(exponent, axis=-1, keepdims=True))
        weights_low = (exponent / row_sum).astype(jnp.bfloat16)
        mixed_block = jnp.einsum('hqk,khd->qhd', weights_low.astype(jnp.float32), value_rows.astype(jnp.float32))
        return (mixed_block.astype(jnp.bfloat16), (row_peak + jnp.log(row_sum))[..., 0])
    mixed_rows, log_sums = lax.map(one_block, jnp.arange(row_total // block_rows, dtype=jnp.int32))
    return (mixed_rows.reshape(row_total, head_count, head_width), log_sums)

def attention_backward(query_rows, key_rows, value_rows, mixed_rows, grad_mixed, log_sums, segments):
    row_total, head_count, head_width = query_rows.shape
    block_rows = min(512, row_total)
    score_scale = head_width ** (-0.5)

    def one_block(running, block_index):
        grad_keys, grad_values = running
        scores, query_block, first_row = block_scores(query_rows, key_rows, segments, block_index, block_rows)
        weights = jnp.exp(scores - log_sums[block_index][..., None])
        weights_low = weights.astype(jnp.bfloat16)
        grad_block = lax.dynamic_slice_in_dim(grad_mixed, first_row, block_rows, 0)
        mixed_block = lax.dynamic_slice_in_dim(mixed_rows, first_row, block_rows, 0)
        row_delta = lax.optimization_barrier(jnp.sum(grad_block.astype(jnp.float32) * mixed_block.astype(jnp.float32), axis=-1)).T
        grad_values = grad_values + jnp.einsum('hqk,qhd->khd', weights_low.astype(jnp.float32), grad_block.astype(jnp.float32))
        grad_weights = jnp.einsum('qhd,khd->hqk', grad_block.astype(jnp.float32), value_rows.astype(jnp.float32))
        grad_scores = (weights * (grad_weights - row_delta[..., None]) * score_scale).astype(jnp.bfloat16)
        grad_query = jnp.einsum('hqk,khd->qhd', grad_scores.astype(jnp.float32), key_rows.astype(jnp.float32))
        grad_keys = grad_keys + jnp.einsum('hqk,qhd->khd', grad_scores.astype(jnp.float32), query_block.astype(jnp.float32))
        return ((grad_keys, grad_values), grad_query)
    zero_rows = jnp.zeros((row_total, head_count, head_width), jnp.float32)
    (grad_keys, grad_values), grad_queries = lax.scan(one_block, (zero_rows, zero_rows), jnp.arange(row_total // block_rows, dtype=jnp.int32))
    return (grad_queries.reshape(row_total, head_count, head_width), grad_keys, grad_values)

def reference(tokens, cotangent, lengths, ln1_gain, ln1_bias, qkv_weight, qkv_bias, out_weight, out_bias, ln2_gain, ln2_bias, up_weight, up_bias, down_weight, down_bias):
    norm1_gain = ln1_gain.astype(jnp.float32)
    norm1_offset = ln1_bias.astype(jnp.float32)
    norm2_gain = ln2_gain.astype(jnp.float32)
    norm2_offset = ln2_bias.astype(jnp.float32)
    qkv_flat = qkv_weight.reshape(D, 3 * D)
    bias_flat = jnp.stack([qkv_bias[0].reshape(D).astype(jnp.float32), jnp.zeros((D,), jnp.float32), qkv_bias[1].reshape(D).astype(jnp.float32)]).reshape(3 * D)
    out_shift = out_bias.astype(jnp.float32)
    up_shift = up_bias.reshape(FF).astype(jnp.float32)
    down_shift = down_bias.astype(jnp.float32)

    def group_pass(running, inputs):
        group_tokens, group_cotangent, length_row = inputs
        segments = segment_ids(length_row, ROWS)
        token_float = group_tokens.astype(jnp.float32)
        scaled1, inverse1, pre_one = normalize(token_float, norm1_gain, norm1_offset)
        normed1 = pre_one.astype(jnp.bfloat16)
        projected = (jnp.dot(normed1, qkv_flat, preferred_element_type=jnp.float32) + bias_flat).astype(jnp.bfloat16)
        projected = projected.reshape(ROWS, 3, H, HD)
        queries = projected[:, 0]
        key_rows = projected[:, 1]
        value_rows = projected[:, 2]
        mixed_rows, log_sums = attention_forward(queries, key_rows, value_rows, segments)
        mixed_flat = mixed_rows.reshape(ROWS, D)
        middle = token_float + jnp.dot(mixed_flat, out_weight, preferred_element_type=jnp.float32) + out_shift
        scaled2, inverse2, pre_two = normalize(middle, norm2_gain, norm2_offset)
        normed2 = pre_two.astype(jnp.bfloat16)
        hidden_pre = jnp.dot(normed2, up_weight, preferred_element_type=jnp.float32) + up_shift
        activated = gelu_value(hidden_pre).astype(jnp.bfloat16)
        output = middle + jnp.dot(activated, down_weight, preferred_element_type=jnp.float32) + down_shift
        grad_act = jnp.dot(group_cotangent, down_weight.T, preferred_element_type=jnp.float32)
        grad_down = jnp.dot(activated.T, group_cotangent, preferred_element_type=jnp.float32)
        grad_down_bias = lax.optimization_barrier(jnp.sum(group_cotangent.astype(jnp.float32), axis=0))
        grad_pre = grad_act * gelu_slope(hidden_pre)
        grad_up_bias = lax.optimization_barrier(jnp.sum(grad_pre, axis=0))
        grad_pre_low = grad_pre.astype(jnp.bfloat16)
        grad_up = jnp.dot(normed2.T, grad_pre_low, preferred_element_type=jnp.float32)
        grad_norm2 = jnp.dot(grad_pre_low, up_weight.T, preferred_element_type=jnp.float32)
        grad_ln2_gain = lax.optimization_barrier(jnp.sum(grad_norm2 * scaled2, axis=0))
        grad_ln2_bias = lax.optimization_barrier(jnp.sum(grad_norm2, axis=0))
        grad_middle = group_cotangent.astype(jnp.float32) + normalize_back(grad_norm2, scaled2, inverse2, norm2_gain)
        grad_out_bias = lax.optimization_barrier(jnp.sum(grad_middle, axis=0))
        grad_middle_low = grad_middle.astype(jnp.bfloat16)
        grad_out = jnp.dot(mixed_flat.T, grad_middle_low, preferred_element_type=jnp.float32)
        grad_mixed = jnp.dot(grad_middle_low, out_weight.T, preferred_element_type=jnp.float32).astype(jnp.bfloat16)
        grad_queries, grad_keys, grad_values = attention_backward(queries, key_rows, value_rows, mixed_rows, grad_mixed.reshape(ROWS, H, HD), log_sums, segments)
        grad_bias_qv = jnp.stack([lax.optimization_barrier(jnp.sum(grad_queries, axis=0)), lax.optimization_barrier(jnp.sum(grad_values, axis=0))])
        grad_projected = jnp.stack([grad_queries, grad_keys, grad_values], axis=1).reshape(ROWS, 3 * D).astype(jnp.bfloat16)
        grad_qkv = jnp.dot(normed1.T, grad_projected, preferred_element_type=jnp.float32).reshape(D, 3, D)
        grad_norm1 = jnp.dot(grad_projected, qkv_flat.T, preferred_element_type=jnp.float32)
        grad_ln1_gain = lax.optimization_barrier(jnp.sum(grad_norm1 * scaled1, axis=0))
        grad_ln1_bias = lax.optimization_barrier(jnp.sum(grad_norm1, axis=0))
        grad_inputs = grad_middle + normalize_back(grad_norm1, scaled1, inverse1, norm1_gain)
        terms = (grad_ln1_gain, grad_ln1_bias, grad_qkv, grad_bias_qv, grad_out, grad_out_bias, grad_ln2_gain, grad_ln2_bias, grad_up, grad_up_bias.reshape(FF // HD, HD), grad_down, grad_down_bias)
        running = tuple((total + term for total, term in zip(running, terms)))
        return (running, (output, grad_inputs))
    start_sums = (jnp.zeros((D,), jnp.float32), jnp.zeros((D,), jnp.float32), jnp.zeros((D, 3, D), jnp.float32), jnp.zeros((2, H, HD), jnp.float32), jnp.zeros((D, D), jnp.float32), jnp.zeros((D,), jnp.float32), jnp.zeros((D,), jnp.float32), jnp.zeros((D,), jnp.float32), jnp.zeros((D, FF), jnp.float32), jnp.zeros((FF // HD, HD), jnp.float32), jnp.zeros((FF, D), jnp.float32), jnp.zeros((D,), jnp.float32))
    sums, (outputs, grad_inputs) = lax.scan(group_pass, start_sums, (tokens.reshape(GROUPS, ROWS, D), cotangent.reshape(GROUPS, ROWS, D), lengths))
    return (outputs.reshape(GROUPS * ROWS, D), grad_inputs.reshape(GROUPS * ROWS, D), sums[0], sums[1], sums[2], sums[3], sums[4], sums[5], sums[6], sums[7], sums[8], sums[9], sums[10], sums[11])
```

```python
import math

import jax
import jax.numpy as jnp
from jax import lax
from jax.sharding import PartitionSpec as P

epsilon = 1e-05
gelu_root = math.sqrt(2.0 / math.pi)
gelu_cubic = 0.044715
masked_score = -1e30


def normalize(values, norm_gain, offset):
    center = values - jnp.mean(values, axis=-1, keepdims=True)
    inverse = lax.rsqrt(jnp.mean(center * center, axis=-1, keepdims=True) + epsilon)
    scaled = center * inverse
    return (scaled, inverse, scaled * norm_gain + offset)


def normalize_back(upstream, scaled, inverse, norm_gain):
    weighted = upstream * norm_gain
    return inverse * (
        weighted
        - jnp.mean(weighted, axis=-1, keepdims=True)
        - scaled * jnp.mean(weighted * scaled, axis=-1, keepdims=True)
    )


def gelu_value(values):
    return (
        0.5
        * values
        * (1.0 + jnp.tanh(gelu_root * (values + gelu_cubic * values * values * values)))
    )


def gelu_slope(values):
    tangent = jnp.tanh(gelu_root * (values + gelu_cubic * values * values * values))
    inner_slope = gelu_root * (1.0 + 3.0 * gelu_cubic * values * values)
    return 0.5 * (1.0 + tangent) + 0.5 * values * (1.0 - tangent * tangent) * inner_slope


def segment_ids(length_row, row_total):
    seq_ends = jnp.cumsum(length_row)
    places = jnp.arange(row_total, dtype=jnp.int32)
    return jnp.sum((places[:, None] >= seq_ends[None, :-1]).astype(jnp.int32), axis=1)


def contract_rows(left_rows, right_rows):
    return lax.dot_general(
        left_rows, right_rows, (((0,), (0,)), ((), ())), preferred_element_type=jnp.float32
    )


def contract_cols(left_rows, right_rows):
    return lax.dot_general(
        left_rows, right_rows, (((1,), (1,)), ((), ())), preferred_element_type=jnp.float32
    )


def block_scores(query_rows, key_rows, segments, block_index, block_rows):
    row_total = key_rows.shape[0]
    score_scale = query_rows.shape[2] ** (-0.5)
    places = jnp.arange(row_total, dtype=jnp.int32)
    first_row = block_index * block_rows
    query_block = lax.dynamic_slice_in_dim(query_rows, first_row, block_rows, 0)
    query_segments = lax.dynamic_slice_in_dim(segments, first_row, block_rows, 0)
    query_places = first_row + jnp.arange(block_rows, dtype=jnp.int32)
    allowed = (query_segments[:, None] == segments[None, :]) & (
        places[None, :] <= query_places[:, None]
    )
    scores = (
        jnp.einsum("qhd,khd->hqk", query_block, key_rows, preferred_element_type=jnp.float32)
        * score_scale
    )
    return (jnp.where(allowed[None], scores, masked_score), query_block, first_row)


def attention_forward(query_rows, key_rows, value_rows, segments):
    row_total, head_count, head_width = query_rows.shape
    block_rows = min(512, row_total)

    def one_block(block_index):
        scores, query_block, first_row = block_scores(
            query_rows, key_rows, segments, block_index, block_rows
        )
        row_peak = jnp.max(scores, axis=-1, keepdims=True)
        exponent = jnp.exp(scores - row_peak)
        row_sum = jnp.sum(exponent, axis=-1, keepdims=True)
        weights_low = (exponent / row_sum).astype(jnp.bfloat16)
        mixed_block = jnp.einsum(
            "hqk,khd->qhd", weights_low, value_rows, preferred_element_type=jnp.float32
        )
        return (mixed_block.astype(jnp.bfloat16), (row_peak + jnp.log(row_sum))[..., 0])

    mixed_rows, log_sums = lax.map(one_block, jnp.arange(row_total // block_rows, dtype=jnp.int32))
    return (mixed_rows.reshape(row_total, head_count, head_width), log_sums)


def attention_backward(
    query_rows, key_rows, value_rows, mixed_rows, grad_mixed, log_sums, segments
):
    row_total, head_count, head_width = query_rows.shape
    block_rows = min(512, row_total)
    score_scale = head_width ** (-0.5)

    def one_block(running, block_index):
        grad_keys, grad_values = running
        scores, query_block, first_row = block_scores(
            query_rows, key_rows, segments, block_index, block_rows
        )
        weights = jnp.exp(scores - log_sums[block_index][..., None])
        weights_low = weights.astype(jnp.bfloat16)
        grad_block = lax.dynamic_slice_in_dim(grad_mixed, first_row, block_rows, 0)
        mixed_block = lax.dynamic_slice_in_dim(mixed_rows, first_row, block_rows, 0)
        row_delta = jnp.sum(
            grad_block.astype(jnp.float32) * mixed_block.astype(jnp.float32), axis=-1
        ).T
        grad_values = grad_values + jnp.einsum(
            "hqk,qhd->khd", weights_low, grad_block, preferred_element_type=jnp.float32
        )
        grad_weights = jnp.einsum(
            "qhd,khd->hqk", grad_block, value_rows, preferred_element_type=jnp.float32
        )
        grad_scores = (weights * (grad_weights - row_delta[..., None]) * score_scale).astype(
            jnp.bfloat16
        )
        grad_query = jnp.einsum(
            "hqk,khd->qhd", grad_scores, key_rows, preferred_element_type=jnp.float32
        )
        grad_keys = grad_keys + jnp.einsum(
            "hqk,qhd->khd", grad_scores, query_block, preferred_element_type=jnp.float32
        )
        return ((grad_keys, grad_values), grad_query)

    zero_rows = jnp.zeros((row_total, head_count, head_width), jnp.float32)
    (grad_keys, grad_values), grad_queries = lax.scan(
        one_block, (zero_rows, zero_rows), jnp.arange(row_total // block_rows, dtype=jnp.int32)
    )
    return (grad_queries.reshape(row_total, head_count, head_width), grad_keys, grad_values)


def axis_bits(size):
    count = size.bit_length() - 1
    assert size == 1 << count
    return count


def flip(value, axis_name, bit):
    size = lax.axis_size(axis_name)
    return lax.ppermute(value, axis_name, [(i, i ^ (1 << bit)) for i in range(size)])


def bit_of(axis_name, bit):
    return (lax.axis_index(axis_name) >> bit) & 1


def link_order(size):
    count = axis_bits(size)
    return list(range(2, count)) + list(range(min(2, count)))[::-1]


def gather_rows(block, axis_name, order):
    current = block
    for bit in order:
        other = flip(current, axis_name, bit)
        mine = bit_of(axis_name, bit)
        current = jnp.where(mine == 0, jnp.stack([current, other]), jnp.stack([other, current]))
    count = len(order)
    places = [count - 1 - order.index(bit) for bit in range(count)][::-1]
    current = current.transpose(*places, *range(count, current.ndim))
    return current.reshape((-1,) + block.shape[1:])


def scatter_rows(whole, axis_name, order):
    size = lax.axis_size(axis_name)
    count = axis_bits(size)
    rows = whole.shape[0] // size
    current = whole.reshape((2,) * count + (rows,) + whole.shape[1:])
    left = list(range(count))[::-1]
    for step, bit in enumerate(order):
        place = left.index(bit)
        mine = bit_of(axis_name, bit)
        sent = lax.dynamic_index_in_dim(current, 1 - mine, place, keepdims=False)
        kept = lax.dynamic_index_in_dim(current, mine, place, keepdims=False)
        other = flip(sent.astype(jnp.bfloat16), axis_name, bit)
        current = kept.astype(jnp.float32) + other.astype(jnp.float32)
        if step + 1 < len(order):
            current = current.astype(jnp.bfloat16)
        left.remove(bit)
    return current


def sum_over(value, axis_name):
    for bit in range(axis_bits(lax.axis_size(axis_name))):
        value = value + flip(value, axis_name, bit)
    return value


def as_columns(values, rows):
    flat = values.reshape(-1)
    columns = -(-flat.shape[0] // rows)
    return jnp.pad(flat, (0, columns * rows - flat.shape[0])).reshape(columns, rows)


def shards(
    tokens,
    cotangent,
    lengths,
    ln1_gain,
    ln1_bias,
    qkv_weight,
    qkv_bias,
    out_weight,
    out_bias,
    ln2_gain,
    ln2_bias,
    up_weight,
    up_bias,
    down_weight,
    down_bias,
):
    dp, tp = lax.axis_size("dp"), lax.axis_size("tensor")
    dp_order = link_order(dp)
    tp_order = list(range(axis_bits(tp)))
    local_rows, model_width = tokens.shape
    group_rows = local_rows * tp
    shard_rows = model_width // dp
    head_local = qkv_bias.shape[1]
    head_width = qkv_bias.shape[2] * dp
    local_width = head_local * head_width
    hidden = up_weight.shape[1]

    vectors = jnp.stack([ln1_gain, ln1_bias, out_bias, ln2_gain, ln2_bias, down_bias])
    qkv_cols = as_columns(qkv_bias, shard_rows)
    up_cols = as_columns(up_bias, shard_rows)
    small = jnp.concatenate([vectors, qkv_cols, up_cols])
    small_width = -(-small.shape[0] // 128) * 128
    small = jnp.pad(small, ((0, small_width - small.shape[0]), (0, 0))).T
    qkv_flat_shard = qkv_weight.reshape(shard_rows, 3 * local_width)

    tokens_full = gather_rows(tokens, "tensor", tp_order)
    first = gather_rows(jnp.concatenate([qkv_flat_shard, small], axis=1), "dp", dp_order)
    qkv_flat = first[:, : 3 * local_width]
    small_full = first[:, 3 * local_width :]
    second = gather_rows(jnp.concatenate([out_weight.T, up_weight], axis=1), "dp", dp_order)
    out_t = second[:, :local_width]
    up_full = second[:, local_width:]
    down_t = gather_rows(down_weight.T, "dp", dp_order)
    cotangent_full = gather_rows(cotangent, "tensor", tp_order)

    wide = small_full.astype(jnp.float32).T
    norm1_gain, norm1_offset, out_shift, norm2_gain, norm2_offset, down_shift = (
        wide[i] for i in range(6)
    )
    qkv_at, up_at = 6, 6 + qkv_cols.shape[0]
    up_end = up_at + up_cols.shape[0]

    def from_columns(columns, like):
        count = columns.shape[0]
        blocks = columns.reshape(count, dp, shard_rows).transpose(1, 0, 2).reshape(dp, -1)
        return blocks[:, : like.size].reshape((dp,) + like.shape)

    qkv_bias_full = from_columns(wide[qkv_at:up_at], qkv_bias)
    qkv_bias_full = qkv_bias_full.transpose(1, 2, 0, 3).reshape(2, local_width)
    up_shift = from_columns(wide[up_at:up_end], up_bias).transpose(1, 0, 2).reshape(hidden)
    bias_flat = jnp.concatenate(
        [qkv_bias_full[0], jnp.zeros((local_width,), jnp.float32), qkv_bias_full[1]]
    )

    segments = segment_ids(lengths[0], group_rows)
    token_float = tokens.astype(jnp.float32)
    scaled1, inverse1, _ = normalize(token_float, norm1_gain, norm1_offset)
    scaled1_full, _, pre_one = normalize(tokens_full.astype(jnp.float32), norm1_gain, norm1_offset)
    normed1 = pre_one.astype(jnp.bfloat16)
    projected = (jnp.dot(normed1, qkv_flat, preferred_element_type=jnp.float32) + bias_flat).astype(
        jnp.bfloat16
    )
    projected = projected.reshape(group_rows, 3, head_local, head_width)
    queries = projected[:, 0]
    key_rows = projected[:, 1]
    value_rows = projected[:, 2]
    mixed_rows, log_sums = attention_forward(queries, key_rows, value_rows, segments)
    mixed_flat = mixed_rows.reshape(group_rows, local_width)
    middle = (
        token_float
        + scatter_rows(contract_cols(mixed_flat, out_t), "tensor", tp_order[::-1])
        + out_shift
    )
    scaled2, inverse2, pre_two = normalize(middle, norm2_gain, norm2_offset)
    normed2 = gather_rows(pre_two.astype(jnp.bfloat16), "tensor", tp_order)
    hidden_pre = jnp.dot(normed2, up_full, preferred_element_type=jnp.float32) + up_shift
    activated = gelu_value(hidden_pre).astype(jnp.bfloat16)
    output = (
        middle
        + scatter_rows(contract_cols(activated, down_t), "tensor", tp_order[::-1])
        + down_shift
    )
    grad_down_bias = jnp.sum(cotangent.astype(jnp.float32), axis=0)
    grad_act = jnp.dot(cotangent_full, down_t, preferred_element_type=jnp.float32)
    grad_down_t = contract_rows(cotangent_full, activated)
    grad_pre = grad_act * gelu_slope(hidden_pre)
    grad_up_bias = jnp.sum(grad_pre, axis=0)
    grad_pre_low = grad_pre.astype(jnp.bfloat16)
    grad_up = contract_rows(normed2, grad_pre_low)
    grad_norm2 = scatter_rows(contract_cols(grad_pre_low, up_full), "tensor", tp_order[::-1])
    grad_ln2_gain = jnp.sum(grad_norm2 * scaled2, axis=0)
    grad_ln2_bias = jnp.sum(grad_norm2, axis=0)
    grad_middle = cotangent.astype(jnp.float32) + normalize_back(
        grad_norm2, scaled2, inverse2, norm2_gain
    )
    grad_out_bias = jnp.sum(grad_middle, axis=0)
    grad_middle_full = gather_rows(grad_middle.astype(jnp.bfloat16), "tensor", tp_order)
    down_shard = scatter_rows(grad_down_t.astype(jnp.bfloat16), "dp", dp_order[::-1])
    up_shard = scatter_rows(grad_up.astype(jnp.bfloat16), "dp", dp_order[::-1])
    grad_out_t = contract_rows(grad_middle_full, mixed_flat)
    out_shard = scatter_rows(grad_out_t.astype(jnp.bfloat16), "dp", dp_order[::-1])
    grad_mixed = jnp.dot(grad_middle_full, out_t, preferred_element_type=jnp.float32).astype(jnp.bfloat16)
    grad_queries, grad_keys, grad_values = attention_backward(
        queries,
        key_rows,
        value_rows,
        mixed_rows,
        grad_mixed.reshape(group_rows, head_local, head_width),
        log_sums,
        segments,
    )
    grad_bias_qv = jnp.stack([jnp.sum(grad_queries, axis=0), jnp.sum(grad_values, axis=0)])
    grad_projected = (
        jnp.stack([grad_queries, grad_keys, grad_values], axis=1)
        .reshape(group_rows, 3 * local_width)
        .astype(jnp.bfloat16)
    )
    grad_part1 = contract_cols(grad_projected, qkv_flat)
    grad_norm1 = scatter_rows(grad_part1, "tensor", tp_order[::-1])
    grad_ln1_gain = jnp.sum(grad_part1 * scaled1_full, axis=0)
    grad_ln1_bias = jnp.sum(grad_part1, axis=0)
    grad_qkv = contract_rows(normed1, grad_projected)

    def to_columns(values, count):
        padded = jnp.pad(values, ((0, 0), (0, count * shard_rows - values.shape[1])))
        return padded.reshape(dp, count, shard_rows).transpose(1, 0, 2).reshape(count, model_width)

    qkv_grads = grad_bias_qv.reshape(2, head_local, dp, -1).transpose(2, 0, 1, 3).reshape(dp, -1)
    up_grads = grad_up_bias.reshape(up_bias.shape[0], dp, -1).transpose(1, 0, 2).reshape(dp, -1)
    sums = jnp.concatenate(
        [
            jnp.stack(
                [
                    grad_ln1_gain,
                    grad_ln1_bias,
                    grad_out_bias,
                    grad_ln2_gain,
                    grad_ln2_bias,
                    grad_down_bias,
                ]
            ),
            to_columns(qkv_grads, up_at - qkv_at),
            to_columns(up_grads, up_end - up_at),
        ]
    ).astype(jnp.bfloat16)
    sums = jnp.pad(sums, ((0, small_width - sums.shape[0]), (0, 0))).T
    last = scatter_rows(
        jnp.concatenate([grad_qkv.astype(jnp.bfloat16), sums], axis=1), "dp", dp_order[::-1]
    )
    qkv_shard = last[:, : 3 * local_width].reshape(shard_rows, 3, local_width)
    sums_own = last[:, 3 * local_width :].T[:up_end]
    vector_sums = sum_over(sums_own[:6], "tensor")
    grad_tokens = grad_middle + normalize_back(grad_norm1, scaled1, inverse1, norm1_gain)
    return (
        output,
        grad_tokens,
        vector_sums[0],
        vector_sums[1],
        qkv_shard,
        sums_own[qkv_at:up_at].reshape(-1)[: qkv_bias.size].reshape(qkv_bias.shape),
        out_shard.T,
        vector_sums[2],
        vector_sums[3],
        vector_sums[4],
        up_shard,
        sums_own[up_at:up_end].reshape(-1)[: up_bias.size].reshape(up_bias.shape),
        down_shard.T,
        vector_sums[5],
    )


def solution(mesh):
    in_specs = (
        P(("dp", "tensor"), None),
        P(("dp", "tensor"), None),
        P("dp", None),
        P("dp"),
        P("dp"),
        P("dp", None, "tensor"),
        P(None, "tensor", "dp"),
        P("tensor", "dp"),
        P("dp"),
        P("dp"),
        P("dp"),
        P("dp", "tensor"),
        P("tensor", "dp"),
        P("tensor", "dp"),
        P("dp"),
    )
    out_specs = (
        P(("dp", "tensor"), None),
        P(("dp", "tensor"), None),
        P("dp"),
        P("dp"),
        P("dp", None, "tensor"),
        P(None, "tensor", "dp"),
        P("tensor", "dp"),
        P("dp"),
        P("dp"),
        P("dp"),
        P("dp", "tensor"),
        P("tensor", "dp"),
        P("tensor", "dp"),
        P("dp"),
    )
    return jax.shard_map(shards, mesh=mesh, in_specs=in_specs, out_specs=out_specs, check_vma=False)
```

```python
import functools
import math

import jax
import jax.numpy as jnp
from jax import lax
from jax.experimental import pallas as pl
from jax.experimental.pallas import tpu as pltpu
from jax.sharding import PartitionSpec as P

epsilon = 1e-05
gelu_root = math.sqrt(2.0 / math.pi)
gelu_cubic = 0.044715
masked_score = -1e30


def normalize(values, norm_gain, offset):
    center = values - jnp.mean(values, axis=-1, keepdims=True)
    inverse = lax.rsqrt(jnp.mean(center * center, axis=-1, keepdims=True) + epsilon)
    scaled = center * inverse
    return (scaled, inverse, scaled * norm_gain + offset)


def normalize_back(upstream, scaled, inverse, norm_gain):
    weighted = upstream * norm_gain
    return inverse * (
        weighted
        - jnp.mean(weighted, axis=-1, keepdims=True)
        - scaled * jnp.mean(weighted * scaled, axis=-1, keepdims=True)
    )


def gelu_value(values):
    return (
        0.5
        * values
        * (1.0 + jnp.tanh(gelu_root * (values + gelu_cubic * values * values * values)))
    )


def gelu_slope(values):
    tangent = jnp.tanh(gelu_root * (values + gelu_cubic * values * values * values))
    inner_slope = gelu_root * (1.0 + 3.0 * gelu_cubic * values * values)
    return 0.5 * (1.0 + tangent) + 0.5 * values * (1.0 - tangent * tangent) * inner_slope


def contract_rows(left_rows, right_rows):
    return lax.dot_general(
        left_rows, right_rows, (((0,), (0,)), ((), ())), preferred_element_type=jnp.float32
    )


def contract_cols(left_rows, right_rows):
    return lax.dot_general(
        left_rows, right_rows, (((1,), (1,)), ((), ())), preferred_element_type=jnp.float32
    )


def lane_pair(rows, width):
    lane = lax.broadcasted_iota(jnp.int32, rows.shape, 1)
    zero = jnp.zeros_like(rows)
    first = jnp.where(lane < width, rows, zero)
    second = jnp.where(lane < width, zero, rows)
    return jnp.concatenate([first, second], axis=0)


def nt(left, right):
    return lax.dot_general(
        left, right, (((1,), (1,)), ((), ())), preferred_element_type=jnp.float32
    )


def nn(left, right):
    return lax.dot_general(
        left, right, (((1,), (0,)), ((), ())), preferred_element_type=jnp.float32
    )


def tile_pairs(group_rows, block, longest):
    count = group_rows // block
    first = [max(0, (i * block - longest + 1) // block) for i in range(count)]
    return [[j for j in range(first[i], i + 1)] for i in range(count)]


def fill_masks(lengths_ref, mask_ref, tiles, block):
    at = 0
    for i, keys in enumerate(tiles):
        query = i * block + lax.broadcasted_iota(jnp.int32, (1, block), 1)
        start = jnp.zeros((1, block), jnp.int32)
        end = jnp.int32(0)
        for s in range(lengths_ref.shape[1] - 1):
            end = end + lengths_ref[0, s]
            start = jnp.where(query >= end, end, start)
        for j in keys:
            key = j * block + lax.broadcasted_iota(jnp.int32, (block, block), 0)
            allowed = (key >= start) & (key <= query)
            mask_ref[at] = jnp.where(allowed, 0.0, masked_score).astype(jnp.float32)
            at += 1


def unpair(both, block, width):
    own = jnp.concatenate([both[:width, :block], both[width:, block:]], axis=0)
    return own.T


def attention_kernel(lengths_ref, x_ref, o_ref, lse_ref, mask_ref, vt_ref, *, tiles, block, width, scale):
    @pl.when(pl.program_id(0) == 0)
    def _():
        fill_masks(lengths_ref, mask_ref, tiles, block)

    pair = 2 * width
    vt_ref[...] = x_ref[:, 2 * pair : 3 * pair].T
    lse_ref[...] = jnp.zeros_like(lse_ref)
    at = 0
    for i, keys in enumerate(tiles):
        rows = slice(i * block, (i + 1) * block)
        queries = lane_pair(x_ref[rows, :pair], width)
        parts = []
        for t, j in enumerate(keys):
            score = nt(x_ref[j * block : (j + 1) * block, pair : 2 * pair], queries) * scale
            mask = mask_ref[at + t]
            parts.append(score + jnp.concatenate([mask, mask], axis=1))
        at += len(keys)
        peak = parts[0].max(axis=0, keepdims=True)
        for part in parts[1:]:
            peak = jnp.maximum(peak, part.max(axis=0, keepdims=True))
        total = jnp.zeros_like(peak)
        mixed = jnp.zeros((pair, 2 * block), jnp.float32)
        for part, j in zip(parts, keys):
            weight = jnp.exp(part - peak)
            total = total + weight.sum(axis=0, keepdims=True)
            mixed = mixed + nn(vt_ref[:, j * block : (j + 1) * block], weight.astype(jnp.bfloat16))
        o_ref[rows, :] = unpair(mixed / total, block, width).astype(o_ref.dtype)
        log_sum = peak + jnp.log(total)
        lse_ref[0:1, rows] = log_sum[:, :block]
        lse_ref[1:2, rows] = log_sum[:, block:]


def attention_back_kernel(
    lengths_ref, x_ref, o_ref, do_ref, lse_ref, g_ref, sum_ref, mask_ref, kt_ref, dk_ref, dv_ref, *, tiles, block, width, scale
):
    @pl.when(pl.program_id(0) == 0)
    def _():
        fill_masks(lengths_ref, mask_ref, tiles, block)

    pair = 2 * width
    kt_ref[...] = x_ref[:, pair : 2 * pair].T
    dk_ref[...] = jnp.zeros_like(dk_ref)
    dv_ref[...] = jnp.zeros_like(dv_ref)
    query_sum = jnp.zeros((1, pair), jnp.float32)
    at = 0
    for i, keys in enumerate(tiles):
        rows = slice(i * block, (i + 1) * block)
        queries = lane_pair(x_ref[rows, :pair], width)
        upstream = do_ref[rows, :]
        product = (upstream.astype(jnp.float32) * o_ref[rows, :].astype(jnp.float32)).T
        delta = jnp.concatenate(
            [
                product[:width].sum(axis=0, keepdims=True),
                product[width:].sum(axis=0, keepdims=True),
            ],
            axis=1,
        )
        log_sum = jnp.concatenate([lse_ref[0:1, rows], lse_ref[1:2, rows]], axis=1)
        upstream = lane_pair(upstream, width)
        grad_query = jnp.zeros((pair, 2 * block), jnp.float32)
        for j in keys:
            at_keys = slice(j * block, (j + 1) * block)
            score = nt(x_ref[at_keys, pair : 2 * pair], queries) * scale
            mask = mask_ref[at]
            at += 1
            weight = jnp.exp(score + jnp.concatenate([mask, mask], axis=1) - log_sum)
            grad_weight = nt(x_ref[at_keys, 2 * pair : 3 * pair], upstream)
            grad_score = (weight * (grad_weight - delta)).astype(jnp.bfloat16)
            dv_ref[at_keys, :] += nn(weight.astype(jnp.bfloat16), upstream)
            dk_ref[at_keys, :] += nn(grad_score, queries)
            grad_query = grad_query + nn(kt_ref[:, at_keys], grad_score)
        own = unpair(grad_query, block, width) * scale
        query_sum = query_sum + own.sum(axis=0, keepdims=True)
        g_ref[rows, :pair] = own.astype(g_ref.dtype)
    g_ref[:, pair : 2 * pair] = (dk_ref[...] * scale).astype(g_ref.dtype)
    g_ref[:, 2 * pair :] = dv_ref[...].astype(g_ref.dtype)
    sum_ref[...] = jnp.concatenate(
        [query_sum, dv_ref[...].sum(axis=0, keepdims=True), jnp.zeros((6, pair), jnp.float32)], axis=0
    )


def attention(lengths, projected, width):
    group_rows, columns = projected.shape
    pair = 2 * width
    count = columns // (3 * pair)
    block = min(256, group_rows)
    tiles = tile_pairs(group_rows, block, group_rows // 2)
    total = sum(len(keys) for keys in tiles)
    return pl.pallas_call(
        functools.partial(attention_kernel, tiles=tiles, block=block, width=width, scale=width**-0.5),
        out_shape=(
            jax.ShapeDtypeStruct((group_rows, count * pair), jnp.bfloat16),
            jax.ShapeDtypeStruct((count * 8, group_rows), jnp.float32),
        ),
        grid=(count,),
        in_specs=[
            pl.BlockSpec(memory_space=pltpu.SMEM),
            pl.BlockSpec((group_rows, 3 * pair), lambda p: (0, p)),
        ],
        out_specs=(
            pl.BlockSpec((group_rows, pair), lambda p: (0, p)),
            pl.BlockSpec((8, group_rows), lambda p: (p, 0)),
        ),
        scratch_shapes=[
            pltpu.VMEM((total, block, block), jnp.float32),
            pltpu.VMEM((pair, group_rows), jnp.bfloat16),
        ],
        compiler_params=pltpu.CompilerParams(vmem_limit_bytes=56 << 20),
        name="attention",
    )(lengths, projected)


def attention_back(lengths, projected, mixed, grad_mixed, log_sums, width):
    group_rows, columns = projected.shape
    pair = 2 * width
    count = columns // (3 * pair)
    block = min(256, group_rows)
    tiles = tile_pairs(group_rows, block, group_rows // 2)
    total = sum(len(keys) for keys in tiles)
    return pl.pallas_call(
        functools.partial(
            attention_back_kernel, tiles=tiles, block=block, width=width, scale=width**-0.5
        ),
        out_shape=(
            jax.ShapeDtypeStruct((group_rows, columns), jnp.bfloat16),
            jax.ShapeDtypeStruct((8, count * pair), jnp.float32),
        ),
        grid=(count,),
        in_specs=[
            pl.BlockSpec(memory_space=pltpu.SMEM),
            pl.BlockSpec((group_rows, 3 * pair), lambda p: (0, p)),
            pl.BlockSpec((group_rows, pair), lambda p: (0, p)),
            pl.BlockSpec((group_rows, pair), lambda p: (0, p)),
            pl.BlockSpec((8, group_rows), lambda p: (p, 0)),
        ],
        out_specs=(
            pl.BlockSpec((group_rows, 3 * pair), lambda p: (0, p)),
            pl.BlockSpec((8, pair), lambda p: (0, p)),
        ),
        scratch_shapes=[
            pltpu.VMEM((total, block, block), jnp.float32),
            pltpu.VMEM((pair, group_rows), jnp.bfloat16),
            pltpu.VMEM((group_rows, pair), jnp.float32),
            pltpu.VMEM((group_rows, pair), jnp.float32),
        ],
        compiler_params=pltpu.CompilerParams(vmem_limit_bytes=56 << 20),
        name="attention_back",
    )(lengths, projected, mixed, grad_mixed, log_sums)


def tie(*values):
    return lax.optimization_barrier(values)


def flip(value, axis_name, bit):
    size = lax.axis_size(axis_name)
    return lax.ppermute(value, axis_name, [(i, i ^ (1 << bit)) for i in range(size)])


def shift(value, axis_name, step, amount):
    size = lax.axis_size(axis_name)
    return lax.ppermute(value, axis_name, [(i, (i + amount * step) % size) for i in range(size)])


def place_kernel(where_ref, *refs):
    pieces, out_ref, sems = refs[:-2], refs[-2], refs[-1]
    line = pieces[0].shape[0]
    copies = []
    for p, piece in enumerate(pieces):
        for k in range(line):
            at = where_ref[p * line + k]
            copies.append(
                pltpu.make_async_copy(piece.at[k], out_ref.at[at], sems.at[p * line + k])
            )
    for copy in copies:
        copy.start()
    for copy in copies:
        copy.wait()


def place_blocks(pieces, where):
    line, rows, columns = pieces[0].shape
    blocks = line * len(pieces)
    out = pl.pallas_call(
        place_kernel,
        out_shape=jax.ShapeDtypeStruct((blocks, rows, columns), pieces[0].dtype),
        in_specs=[pl.BlockSpec(memory_space=pltpu.SMEM)]
        + [pl.BlockSpec(memory_space=pl.ANY)] * len(pieces),
        out_specs=pl.BlockSpec(memory_space=pltpu.VMEM),
        scratch_shapes=[pltpu.SemaphoreType.DMA((blocks,))],
        name="place_blocks",
    )
    out = out(where, *pieces)
    return out.reshape(blocks * rows, columns)


def gather_line(block):
    line = lax.axis_size("dp") // 4
    return [block] + [shift(block, "dp", 4, k) for k in range(1, line)]


def gather_rest(blocks):
    line = len(blocks)
    own = jnp.stack(blocks)
    side = flip(own, "dp", 1)
    index = lax.axis_index("dp")
    pieces = [own, side] + [flip(half, "dp", 0) for half in (own, side)]
    back = (index // 4 - jnp.arange(line)) % line
    where = jnp.concatenate([back * 4 + ((index % 4) ^ mask) for mask in (0, 2, 1, 3)])
    return place_blocks(pieces, where.astype(jnp.int32))


def pick(values, at, axis):
    return lax.dynamic_index_in_dim(values, at, axis, keepdims=False)


def scatter_core(wholes):
    size = lax.axis_size("dp")
    core = lax.axis_index("dp") % 2
    blocks = [
        whole.reshape(size // 4, 2, 2, whole.shape[0] // size, whole.shape[1]) for whole in wholes
    ]

    def taken(at):
        return jnp.concatenate([pick(block, at, 2) for block in blocks], axis=-1)

    return taken(core), flip(taken(1 - core), "dp", 0)


def scatter_side(kept, met):
    side = (lax.axis_index("dp") // 2) % 2

    def summed(at):
        return pick(kept, at, 1).astype(jnp.float32) + pick(met, at, 1).astype(jnp.float32)

    return summed(side), flip(summed(1 - side).astype(jnp.bfloat16), "dp", 1)


def scatter_line(mine, crossed):
    line = mine.shape[0]
    at = lax.axis_index("dp") // 4
    sums = mine + crossed.astype(jnp.float32)
    low = sums.astype(jnp.bfloat16)
    return [pick(sums, at, 0)] + [
        shift(pick(low, (at + k) % line, 0), "dp", 4, k) for k in range(1, line)
    ]


def total_of(parts):
    return sum(part.astype(jnp.float32) for part in parts)


def bits_of(size):
    count = size.bit_length() - 1
    assert size == 1 << count
    return count


def relative(whole):
    size = lax.axis_size("tensor")
    blocks = whole.reshape((size, whole.shape[0] // size) + whole.shape[1:])
    return [pick(blocks, lax.axis_index("tensor") ^ j, 0) for j in range(size)]


def gather_tensor(block):
    current = block
    for bit in range(bits_of(lax.axis_size("tensor"))):
        current = jnp.concatenate([current, flip(current, "tensor", bit)])
    return current[block.shape[0] :]


def scatter_tensor(own, rest):
    rows = own.shape[0]
    blocks = [own] + [rest[at : at + rows] for at in range(0, rest.shape[0], rows)]
    for bit in reversed(range(bits_of(lax.axis_size("tensor")))):
        half = len(blocks) // 2
        sent = blocks[half:]
        sent = sent[0] if half == 1 else jnp.concatenate(sent)
        met = flip(sent.astype(jnp.bfloat16), "tensor", bit)
        blocks = [
            block + met[j * rows : (j + 1) * rows].astype(jnp.float32)
            for j, block in enumerate(blocks[:half])
        ]
    return blocks[0]


def sum_over(value, axis_name):
    for bit in range(bits_of(lax.axis_size(axis_name))):
        value = value + flip(value, axis_name, bit)
    return value


def as_columns(values, rows):
    flat = values.reshape(-1)
    columns = -(-flat.shape[0] // rows)
    return jnp.pad(flat, (0, columns * rows - flat.shape[0])).reshape(columns, rows)


def block(
    tokens,
    cotangent,
    lengths,
    ln1_gain,
    ln1_bias,
    qkv_weight,
    qkv_bias,
    out_weight,
    out_bias,
    ln2_gain,
    ln2_bias,
    up_weight,
    up_bias,
    down_weight,
    down_bias,
):
    dp, tp = lax.axis_size("dp"), lax.axis_size("tensor")
    local_rows, model_width = tokens.shape
    shard_rows = model_width // dp
    head_local = qkv_bias.shape[1]
    head_width = qkv_bias.shape[2] * dp
    local_width = head_local * head_width
    pairs = head_local // 2
    hidden = up_weight.shape[1]

    vectors = jnp.stack([ln1_gain, ln1_bias, out_bias, ln2_gain, ln2_bias, down_bias])
    qkv_cols = as_columns(qkv_bias, shard_rows)
    up_cols = as_columns(up_bias, shard_rows)
    small = jnp.concatenate([vectors, qkv_cols, up_cols])
    small_width = -(-small.shape[0] // 128) * 128
    small = jnp.pad(small, ((0, small_width - small.shape[0]), (0, 0))).T
    parts = 2 if pairs % 2 == 0 else 1
    part_cols = 3 * local_width // parts
    qkv_shard = (
        qkv_weight.reshape(shard_rows, 3, pairs, 2 * head_width)
        .transpose(0, 2, 1, 3)
        .reshape(shard_rows, parts, part_cols)
    )
    columns = [[qkv_shard[:, part]] for part in range(parts)]
    columns[0].append(small)
    columns[-1].append(out_weight.T)
    shard_list = [jnp.concatenate(piece, axis=1) for piece in columns]
    up_shard, down_shard = up_weight, down_weight.T

    half = local_rows // 2
    rest_rows = [gather_tensor(tokens[:half])]
    lines = [gather_line(shard_list[0])]
    late_tokens, _ = tie(tokens[half:], rest_rows[0])
    for piece in shard_list[1:]:
        piece, *_ = tie(piece, rest_rows[0], *lines[-1])
        lines.append(gather_line(piece))
    rest_rows.append(gather_tensor(late_tokens))
    others = [part.reshape(tp - 1, half, model_width) for part in rest_rows]
    tokens_rest = jnp.concatenate(others, axis=1).reshape((tp - 1) * local_rows, model_width)
    cotangent_late, tokens_rest = tie(cotangent, tokens_rest)
    cotangent_rest = gather_tensor(cotangent_late)

    rest = [gather_rest(lines[0])]
    small_full = rest[0][:, part_cols : part_cols + small_width]

    wide = small_full.astype(jnp.float32).T
    norm1_gain, norm1_offset, out_shift, norm2_gain, norm2_offset, down_shift = (
        wide[i] for i in range(6)
    )
    qkv_at, up_at = 6, 6 + qkv_cols.shape[0]
    up_end = up_at + up_cols.shape[0]

    def from_columns(columns, like):
        count = columns.shape[0]
        blocks = columns.reshape(count, dp, shard_rows).transpose(1, 0, 2).reshape(dp, -1)
        return blocks[:, : like.size].reshape((dp,) + like.shape)

    qkv_bias_full = from_columns(wide[qkv_at:up_at], qkv_bias)
    qkv_bias_full = qkv_bias_full.transpose(1, 2, 0, 3).reshape(2, pairs, 2 * head_width)
    bias_parts = jnp.stack(
        [qkv_bias_full[0], jnp.zeros_like(qkv_bias_full[0]), qkv_bias_full[1]], axis=1
    ).reshape(parts, part_cols)
    up_shift = from_columns(wide[up_at:up_end], up_bias).transpose(1, 0, 2).reshape(hidden)

    token_float = tokens.astype(jnp.float32)
    scaled1, inverse1, pre_own = normalize(token_float, norm1_gain, norm1_offset)
    scaled1_rest, _, pre_rest = normalize(
        tokens_rest.astype(jnp.float32), norm1_gain, norm1_offset
    )
    normed1 = jnp.concatenate(
        relative(jnp.concatenate([pre_own.astype(jnp.bfloat16), pre_rest.astype(jnp.bfloat16)]))
    )

    def project(piece, bias):
        weight = piece[:, :part_cols]
        values = jnp.dot(normed1, weight, preferred_element_type=jnp.float32) + bias
        return weight, values.astype(jnp.bfloat16)

    up_piece, down_piece = up_shard, down_shard
    weight, part = project(rest[0], bias_parts[0])
    up_piece, *_ = tie(up_piece, *lines[-1])
    up_line = gather_line(up_piece)
    qkv_parts, projected = [weight], [part]
    for line, bias in zip(lines[1:], bias_parts[1:]):
        rest.append(gather_rest(line))
        weight, part = project(rest[-1], bias)
        qkv_parts.append(weight)
        projected.append(part)
    out_t = rest[-1][:, -local_width:]
    down_piece, *_ = tie(down_piece, *up_line)
    projected[-1], cotangent_rest = tie(projected[-1], cotangent_rest)
    down_line = gather_line(down_piece)
    attended = []
    for part in projected:
        attended.append(attention(lengths, part, head_width))
    mixed = jnp.concatenate([part[0] for part in attended], axis=1)
    mixed_own, *mixed_rest = relative(mixed)
    mixed_rest = jnp.concatenate(mixed_rest)
    up_full = gather_rest(up_line)
    out_rest = contract_cols(mixed_rest, out_t).astype(jnp.bfloat16)
    (out_own,) = tie(contract_cols(mixed_own, out_t))
    attended_out = scatter_tensor(out_own, out_rest)
    down_t = gather_rest(down_line)
    middle = token_float + attended_out + out_shift

    scaled2, inverse2, pre_two = normalize(middle, norm2_gain, norm2_offset)
    normed2_own = pre_two.astype(jnp.bfloat16)
    normed2_rest = gather_tensor(normed2_own)

    def feed_forward(normed, upstream):
        pre = jnp.dot(normed, up_full, preferred_element_type=jnp.float32) + up_shift
        grad_pre = jnp.dot(upstream, down_t, preferred_element_type=jnp.float32) * gelu_slope(pre)
        low = grad_pre.astype(jnp.bfloat16)
        return gelu_value(pre).astype(jnp.bfloat16), low, jnp.sum(grad_pre, axis=0)

    act_own, pre_own, up_sum_own = tie(*feed_forward(normed2_own, cotangent))
    act_rest, pre_rest, up_sum_rest = tie(*feed_forward(normed2_rest, cotangent_rest))
    grad_up_bias = up_sum_own + up_sum_rest
    norm_rest = contract_cols(pre_rest, up_full).astype(jnp.bfloat16)
    (norm_own,) = tie(contract_cols(pre_own, up_full))
    grad_norm2 = scatter_tensor(norm_own, norm_rest)
    activated = jnp.concatenate([act_own, act_rest])
    grad_pre_low = jnp.concatenate([pre_own, pre_rest])
    cotangent_all = jnp.concatenate([cotangent, cotangent_rest])
    normed2 = jnp.concatenate([normed2_own, normed2_rest])
    grad_down = contract_rows(cotangent_all, activated).astype(jnp.bfloat16)
    grad_up = contract_rows(normed2, grad_pre_low).astype(jnp.bfloat16)
    down_core = scatter_core([grad_down])
    up_core = scatter_core([grad_up])
    grad_down_bias = jnp.sum(cotangent.astype(jnp.float32), axis=0)
    grad_ln2_gain = jnp.sum(grad_norm2 * scaled2, axis=0)
    grad_ln2_bias = jnp.sum(grad_norm2, axis=0)
    grad_middle = cotangent.astype(jnp.float32) + normalize_back(
        grad_norm2, scaled2, inverse2, norm2_gain
    )
    grad_out_bias = jnp.sum(grad_middle, axis=0)
    grad_middle_own = grad_middle.astype(jnp.bfloat16)
    grad_middle_rest = gather_tensor(grad_middle_own)
    down_side = scatter_side(*down_core)
    result_rest = contract_cols(act_rest, down_t).astype(jnp.bfloat16)
    (result_own,) = tie(contract_cols(act_own, down_t))
    feed = scatter_tensor(result_own, result_rest)
    feed, middle_late = tie(feed, middle)
    output = middle_late + feed + down_shift

    grad_middle_all = jnp.concatenate([grad_middle_own, grad_middle_rest])
    grad_mixed = jnp.dot(grad_middle_all, out_t, preferred_element_type=jnp.float32)
    grad_mixed = jnp.concatenate(relative(grad_mixed.astype(jnp.bfloat16)))
    up_side = scatter_side(*up_core)
    width = local_width // parts
    grad_parts, bias_parts = [], []
    down_own = scatter_line(*down_side)
    up_own = None
    for part in range(parts):
        upstream = grad_mixed[:, part * width : (part + 1) * width]
        if part == parts - 1:
            upstream, *up_side = tie(upstream, *up_side)
            up_own = scatter_line(*up_side)
        grads, bias_sums = attention_back(
            lengths, projected[part], attended[part][0], upstream, attended[part][1], head_width
        )
        grad_parts.append(grads)
        bias_parts.append(bias_sums[:2])
    bias_sums = jnp.concatenate(bias_parts, axis=1)
    grad_out_t = contract_rows(
        grad_middle_all, jnp.concatenate([mixed_own, mixed_rest])
    ).astype(jnp.bfloat16)

    def first_grad(blocks):
        return sum(contract_cols(grads, weight) for grads, weight in zip(blocks, qkv_parts))

    by_owner = [relative(grads) for grads in grad_parts]
    part_rest = first_grad([jnp.concatenate(blocks[1:]) for blocks in by_owner])
    (part_own,) = tie(first_grad([blocks[0] for blocks in by_owner]))
    grad_norm1 = scatter_tensor(part_own, part_rest)
    seen_own, seen_rest = tie(part_own, part_rest)
    grad_ln1_gain, grad_ln1_bias = tie(
        jnp.sum(seen_own * scaled1, axis=0) + jnp.sum(seen_rest * scaled1_rest, axis=0),
        jnp.sum(seen_own, axis=0) + jnp.sum(seen_rest, axis=0),
    )
    grad_qkv = []
    for part, grads in enumerate(grad_parts):
        grad_qkv.append(contract_rows(normed1, grads).astype(jnp.bfloat16))

    def to_columns(values, count):
        padded = jnp.pad(values, ((0, 0), (0, count * shard_rows - values.shape[1])))
        return padded.reshape(dp, count, shard_rows).transpose(1, 0, 2).reshape(count, model_width)

    qkv_grads = bias_sums.reshape(2, head_local, dp, -1).transpose(2, 0, 1, 3).reshape(dp, -1)
    up_grads = grad_up_bias.reshape(up_bias.shape[0], dp, -1).transpose(1, 0, 2).reshape(dp, -1)
    sums = jnp.concatenate(
        [
            jnp.stack(
                [
                    grad_ln1_gain,
                    grad_ln1_bias,
                    grad_out_bias,
                    grad_ln2_gain,
                    grad_ln2_bias,
                    grad_down_bias,
                ]
            ),
            to_columns(qkv_grads, up_at - qkv_at),
            to_columns(up_grads, up_end - up_at),
        ]
    ).astype(jnp.bfloat16)
    sums = jnp.pad(sums, ((0, small_width - sums.shape[0]), (0, 0))).T
    pieces = [[part] for part in grad_qkv]
    pieces[0].append(grad_out_t)
    pieces[-1].append(sums)
    own = []
    for piece in pieces:
        core = scatter_core(piece)
        own.append(total_of(scatter_line(*scatter_side(*core))))
    up_shard, down_shard = total_of(up_own), total_of(down_own)
    out_shard = own[0][:, part_cols : part_cols + local_width]
    sums_own = own[-1][:, -small_width:].T[:up_end]
    qkv_shard = (
        jnp.concatenate([piece[:, :part_cols] for piece in own], axis=1)
        .reshape(shard_rows, pairs, 3, 2 * head_width)
        .transpose(0, 2, 1, 3)
        .reshape(shard_rows, 3, local_width)
    )
    vector_sums = sum_over(sums_own[:6], "tensor")
    grad_tokens = grad_middle + normalize_back(grad_norm1, scaled1, inverse1, norm1_gain)
    return (
        output,
        grad_tokens,
        vector_sums[0],
        vector_sums[1],
        qkv_shard,
        sums_own[qkv_at:up_at].reshape(-1)[: qkv_bias.size].reshape(qkv_bias.shape),
        out_shard.T,
        vector_sums[2],
        vector_sums[3],
        vector_sums[4],
        up_shard,
        sums_own[up_at:up_end].reshape(-1)[: up_bias.size].reshape(up_bias.shape),
        down_shard.T,
        vector_sums[5],
    )


def solution(mesh):
    in_specs = (
        P(("dp", "tensor"), None),
        P(("dp", "tensor"), None),
        P("dp", None),
        P("dp"),
        P("dp"),
        P("dp", None, "tensor"),
        P(None, "tensor", "dp"),
        P("tensor", "dp"),
        P("dp"),
        P("dp"),
        P("dp"),
        P("dp", "tensor"),
        P("tensor", "dp"),
        P("tensor", "dp"),
        P("dp"),
    )
    out_specs = (
        P(("dp", "tensor"), None),
        P(("dp", "tensor"), None),
        P("dp"),
        P("dp"),
        P("dp", None, "tensor"),
        P(None, "tensor", "dp"),
        P("tensor", "dp"),
        P("dp"),
        P("dp"),
        P("dp"),
        P("dp", "tensor"),
        P("tensor", "dp"),
        P("tensor", "dp"),
        P("dp"),
    )
    return jax.shard_map(block, mesh=mesh, in_specs=in_specs, out_specs=out_specs, check_vma=False)
```

```python
import functools
import math

import jax
import jax.numpy as jnp
from jax import lax
from jax.experimental import pallas as pl
from jax.experimental.pallas import tpu as pltpu
from jax.sharding import PartitionSpec as P

epsilon = 1e-05
gelu_root = math.sqrt(2.0 / math.pi)
gelu_cubic = 0.044715
masked_score = -1e30


def normalize(values, norm_gain, offset):
    center = values - jnp.mean(values, axis=-1, keepdims=True)
    inverse = lax.rsqrt(jnp.mean(center * center, axis=-1, keepdims=True) + epsilon)
    scaled = center * inverse
    return (scaled, inverse, scaled * norm_gain + offset)


def normalize_back(upstream, scaled, inverse, norm_gain):
    weighted = upstream * norm_gain
    return inverse * (
        weighted
        - jnp.mean(weighted, axis=-1, keepdims=True)
        - scaled * jnp.mean(weighted * scaled, axis=-1, keepdims=True)
    )


def gelu_value(values):
    return (
        0.5
        * values
        * (1.0 + jnp.tanh(gelu_root * (values + gelu_cubic * values * values * values)))
    )


def gelu_slope(values):
    tangent = jnp.tanh(gelu_root * (values + gelu_cubic * values * values * values))
    inner_slope = gelu_root * (1.0 + 3.0 * gelu_cubic * values * values)
    return 0.5 * (1.0 + tangent) + 0.5 * values * (1.0 - tangent * tangent) * inner_slope


def contract_rows(left_rows, right_rows):
    return lax.dot_general(
        left_rows, right_rows, (((0,), (0,)), ((), ())), preferred_element_type=jnp.float32
    )


def contract_cols(left_rows, right_rows):
    return lax.dot_general(
        left_rows, right_rows, (((1,), (1,)), ((), ())), preferred_element_type=jnp.float32
    )


def lane_pair(rows, width):
    lane = lax.broadcasted_iota(jnp.int32, rows.shape, 1)
    zero = jnp.zeros_like(rows)
    first = jnp.where(lane < width, rows, zero)
    second = jnp.where(lane < width, zero, rows)
    return jnp.concatenate([first, second], axis=0)


def nt(left, right):
    return lax.dot_general(
        left, right, (((1,), (1,)), ((), ())), preferred_element_type=jnp.float32
    )


def nn(left, right):
    return lax.dot_general(
        left, right, (((1,), (0,)), ((), ())), preferred_element_type=jnp.float32
    )


def tile_pairs(group_rows, block, longest):
    count = group_rows // block
    first = [max(0, (i * block - longest + 1) // block) for i in range(count)]
    return [[j for j in range(first[i], i + 1)] for i in range(count)]


def fill_masks(lengths_ref, mask_ref, tiles, block):
    at = 0
    for i, keys in enumerate(tiles):
        query = i * block + lax.broadcasted_iota(jnp.int32, (1, block), 1)
        start = jnp.zeros((1, block), jnp.int32)
        end = jnp.int32(0)
        for s in range(lengths_ref.shape[1] - 1):
            end = end + lengths_ref[0, s]
            start = jnp.where(query >= end, end, start)
        for j in keys:
            key = j * block + lax.broadcasted_iota(jnp.int32, (block, block), 0)
            allowed = (key >= start) & (key <= query)
            mask_ref[at] = jnp.where(allowed, 0.0, masked_score).astype(jnp.float32)
            at += 1


def unpair(both, block, width):
    own = jnp.concatenate([both[:width, :block], both[width:, block:]], axis=0)
    return own.T


def attention_kernel(lengths_ref, x_ref, o_ref, lse_ref, mask_ref, vt_ref, *, tiles, block, width, scale):
    @pl.when(pl.program_id(0) == 0)
    def _():
        fill_masks(lengths_ref, mask_ref, tiles, block)

    pair = 2 * width
    vt_ref[...] = x_ref[:, 2 * pair : 3 * pair].T
    lse_ref[...] = jnp.zeros_like(lse_ref)
    at = 0
    for i, keys in enumerate(tiles):
        rows = slice(i * block, (i + 1) * block)
        queries = lane_pair(x_ref[rows, :pair], width)
        parts = []
        for t, j in enumerate(keys):
            score = nt(x_ref[j * block : (j + 1) * block, pair : 2 * pair], queries) * scale
            mask = mask_ref[at + t]
            parts.append(score + jnp.concatenate([mask, mask], axis=1))
        at += len(keys)
        peak = parts[0].max(axis=0, keepdims=True)
        for part in parts[1:]:
            peak = jnp.maximum(peak, part.max(axis=0, keepdims=True))
        total = jnp.zeros_like(peak)
        mixed = jnp.zeros((pair, 2 * block), jnp.float32)
        for part, j in zip(parts, keys):
            weight = jnp.exp(part - peak)
            total = total + weight.sum(axis=0, keepdims=True)
            mixed = mixed + nn(vt_ref[:, j * block : (j + 1) * block], weight.astype(jnp.bfloat16))
        o_ref[rows, :] = unpair(mixed / total, block, width).astype(o_ref.dtype)
        log_sum = peak + jnp.log(total)
        lse_ref[0:1, rows] = log_sum[:, :block]
        lse_ref[1:2, rows] = log_sum[:, block:]


def attention_back_kernel(
    lengths_ref, x_ref, o_ref, do_ref, lse_ref, g_ref, sum_ref, mask_ref, kt_ref, dk_ref, dv_ref, *, tiles, block, width, scale
):
    @pl.when(pl.program_id(0) == 0)
    def _():
        fill_masks(lengths_ref, mask_ref, tiles, block)

    pair = 2 * width
    kt_ref[...] = x_ref[:, pair : 2 * pair].T
    dk_ref[...] = jnp.zeros_like(dk_ref)
    dv_ref[...] = jnp.zeros_like(dv_ref)
    query_sum = jnp.zeros((1, pair), jnp.float32)
    at = 0
    for i, keys in enumerate(tiles):
        rows = slice(i * block, (i + 1) * block)
        queries = lane_pair(x_ref[rows, :pair], width)
        upstream = do_ref[rows, :]
        product = (upstream.astype(jnp.float32) * o_ref[rows, :].astype(jnp.float32)).T
        delta = jnp.concatenate(
            [
                product[:width].sum(axis=0, keepdims=True),
                product[width:].sum(axis=0, keepdims=True),
            ],
            axis=1,
        )
        log_sum = jnp.concatenate([lse_ref[0:1, rows], lse_ref[1:2, rows]], axis=1)
        upstream = lane_pair(upstream, width)
        grad_query = jnp.zeros((pair, 2 * block), jnp.float32)
        for j in keys:
            at_keys = slice(j * block, (j + 1) * block)
            score = nt(x_ref[at_keys, pair : 2 * pair], queries) * scale
            mask = mask_ref[at]
            at += 1
            weight = jnp.exp(score + jnp.concatenate([mask, mask], axis=1) - log_sum)
            grad_weight = nt(x_ref[at_keys, 2 * pair : 3 * pair], upstream)
            grad_score = (weight * (grad_weight - delta)).astype(jnp.bfloat16)
            dv_ref[at_keys, :] += nn(weight.astype(jnp.bfloat16), upstream)
            dk_ref[at_keys, :] += nn(grad_score, queries)
            grad_query = grad_query + nn(kt_ref[:, at_keys], grad_score)
        own = unpair(grad_query, block, width) * scale
        query_sum = query_sum + own.sum(axis=0, keepdims=True)
        g_ref[rows, :pair] = own.astype(g_ref.dtype)
    g_ref[:, pair : 2 * pair] = (dk_ref[...] * scale).astype(g_ref.dtype)
    g_ref[:, 2 * pair :] = dv_ref[...].astype(g_ref.dtype)
    sum_ref[...] = jnp.concatenate(
        [query_sum, dv_ref[...].sum(axis=0, keepdims=True), jnp.zeros((6, pair), jnp.float32)], axis=0
    )


def attention(lengths, projected, width):
    group_rows, columns = projected.shape
    pair = 2 * width
    count = columns // (3 * pair)
    block = min(256, group_rows)
    tiles = tile_pairs(group_rows, block, group_rows // 2)
    total = sum(len(keys) for keys in tiles)
    return pl.pallas_call(
        functools.partial(attention_kernel, tiles=tiles, block=block, width=width, scale=width**-0.5),
        out_shape=(
            jax.ShapeDtypeStruct((group_rows, count * pair), jnp.bfloat16),
            jax.ShapeDtypeStruct((count * 8, group_rows), jnp.float32),
        ),
        grid=(count,),
        in_specs=[
            pl.BlockSpec(memory_space=pltpu.SMEM),
            pl.BlockSpec((group_rows, 3 * pair), lambda p: (0, p)),
        ],
        out_specs=(
            pl.BlockSpec((group_rows, pair), lambda p: (0, p)),
            pl.BlockSpec((8, group_rows), lambda p: (p, 0)),
        ),
        scratch_shapes=[
            pltpu.VMEM((total, block, block), jnp.float32),
            pltpu.VMEM((pair, group_rows), jnp.bfloat16),
        ],
        compiler_params=pltpu.CompilerParams(vmem_limit_bytes=56 << 20),
        name="attention",
    )(lengths, projected)


def attention_back(lengths, projected, mixed, grad_mixed, log_sums, width):
    group_rows, columns = projected.shape
    pair = 2 * width
    count = columns // (3 * pair)
    block = min(256, group_rows)
    tiles = tile_pairs(group_rows, block, group_rows // 2)
    total = sum(len(keys) for keys in tiles)
    return pl.pallas_call(
        functools.partial(
            attention_back_kernel, tiles=tiles, block=block, width=width, scale=width**-0.5
        ),
        out_shape=(
            jax.ShapeDtypeStruct((group_rows, columns), jnp.bfloat16),
            jax.ShapeDtypeStruct((8, count * pair), jnp.float32),
        ),
        grid=(count,),
        in_specs=[
            pl.BlockSpec(memory_space=pltpu.SMEM),
            pl.BlockSpec((group_rows, 3 * pair), lambda p: (0, p)),
            pl.BlockSpec((group_rows, pair), lambda p: (0, p)),
            pl.BlockSpec((group_rows, pair), lambda p: (0, p)),
            pl.BlockSpec((8, group_rows), lambda p: (p, 0)),
        ],
        out_specs=(
            pl.BlockSpec((group_rows, 3 * pair), lambda p: (0, p)),
            pl.BlockSpec((8, pair), lambda p: (0, p)),
        ),
        scratch_shapes=[
            pltpu.VMEM((total, block, block), jnp.float32),
            pltpu.VMEM((pair, group_rows), jnp.bfloat16),
            pltpu.VMEM((group_rows, pair), jnp.float32),
            pltpu.VMEM((group_rows, pair), jnp.float32),
        ],
        compiler_params=pltpu.CompilerParams(vmem_limit_bytes=56 << 20),
        name="attention_back",
    )(lengths, projected, mixed, grad_mixed, log_sums)


DP, TP = "dp", "tensor"


def tie(*values):
    return lax.optimization_barrier(values)


def flip(value, axis_name, bit):
    size = lax.axis_size(axis_name)
    return lax.ppermute(value, axis_name, [(i, i ^ (1 << bit)) for i in range(size)])


def shift(value, axis_name, step, amount):
    size = lax.axis_size(axis_name)
    return lax.ppermute(value, axis_name, [(i, (i + amount * step) % size) for i in range(size)])


def place_kernel(where_ref, *refs):
    pieces, out_ref, sems = refs[:-2], refs[-2], refs[-1]
    line = pieces[0].shape[0]
    copies = []
    for p, piece in enumerate(pieces):
        for k in range(line):
            at = where_ref[p * line + k]
            copies.append(
                pltpu.make_async_copy(piece.at[k], out_ref.at[at], sems.at[p * line + k])
            )
    for copy in copies:
        copy.start()
    for copy in copies:
        copy.wait()


def place_blocks(pieces, where):
    line, rows, columns = pieces[0].shape
    blocks = line * len(pieces)
    out = pl.pallas_call(
        place_kernel,
        out_shape=jax.ShapeDtypeStruct((blocks, rows, columns), pieces[0].dtype),
        in_specs=[pl.BlockSpec(memory_space=pltpu.SMEM)]
        + [pl.BlockSpec(memory_space=pl.ANY)] * len(pieces),
        out_specs=pl.BlockSpec(memory_space=pltpu.VMEM),
        scratch_shapes=[pltpu.SemaphoreType.DMA((blocks,))],
        name="place_blocks",
    )
    out = out(where, *pieces)
    return out.reshape(blocks * rows, columns)


def gather_line(block):
    line = lax.axis_size(DP) // 4
    return [block] + [shift(block, DP, 4, k) for k in range(1, line)]


def gather_rest(blocks):
    line = len(blocks)
    own = jnp.stack(blocks)
    side = flip(own, DP, 1)
    index = lax.axis_index(DP)
    pieces = [own, side] + [flip(half, DP, 0) for half in (own, side)]
    back = (index // 4 - jnp.arange(line)) % line
    where = jnp.concatenate([back * 4 + ((index % 4) ^ mask) for mask in (0, 2, 1, 3)])
    return place_blocks(pieces, where.astype(jnp.int32))


def pick(values, at, axis):
    return lax.dynamic_index_in_dim(values, at, axis, keepdims=False)


def scatter_core(wholes):
    size = lax.axis_size(DP)
    core, *wholes = tie(lax.axis_index(DP) % 2, *wholes)
    blocks = [
        whole.reshape(size // 4, 2, 2, whole.shape[0] // size, whole.shape[1]) for whole in wholes
    ]

    def taken(at):
        return jnp.concatenate([pick(block, at, 2) for block in blocks], axis=-1)

    return taken(core), flip(taken(1 - core), DP, 0)


def scatter_side(kept, met):
    side = (lax.axis_index(DP) // 2) % 2

    def summed(at):
        return pick(kept, at, 1).astype(jnp.float32) + pick(met, at, 1).astype(jnp.float32)

    sent = summed(1 - side).astype(jnp.bfloat16)
    return summed(side), flip(sent, DP, 1)


def scatter_line(mine, crossed):
    line = mine.shape[0]
    at = lax.axis_index(DP) // 4
    sums = mine + crossed.astype(jnp.float32)
    low = sums.astype(jnp.bfloat16)
    return [pick(sums, at, 0)] + [
        shift(pick(low, (at + k) % line, 0), DP, 4, k) for k in range(1, line)
    ]


def total_of(parts):
    return sum(part.astype(jnp.float32) for part in parts)


def bits_of(size):
    count = size.bit_length() - 1
    assert size == 1 << count
    return count


def relative(whole):
    size = lax.axis_size(TP)
    blocks = whole.reshape((size, whole.shape[0] // size) + whole.shape[1:])
    return [pick(blocks, lax.axis_index(TP) ^ j, 0) for j in range(size)]


def gather_tensor(block):
    current = block
    for bit in range(bits_of(lax.axis_size(TP))):
        current = jnp.concatenate([current, flip(current, TP, bit)])
    return current[block.shape[0] :]


def scatter_tensor(own, rest):
    rows = own.shape[0]
    blocks = [own] + [rest[at : at + rows] for at in range(0, rest.shape[0], rows)]
    for bit in reversed(range(bits_of(lax.axis_size(TP)))):
        half = len(blocks) // 2
        sent = blocks[half:]
        sent = sent[0] if half == 1 else jnp.concatenate(sent)
        met = flip(sent.astype(jnp.bfloat16), TP, bit)
        blocks = [
            block + met[j * rows : (j + 1) * rows].astype(jnp.float32)
            for j, block in enumerate(blocks[:half])
        ]
    return blocks[0]


def sum_over(value, axis_name):
    for bit in range(bits_of(lax.axis_size(axis_name))):
        value = value + flip(value, axis_name, bit)
    return value


def as_columns(values, rows):
    flat = values.reshape(-1)
    columns = -(-flat.shape[0] // rows)
    return jnp.pad(flat, (0, columns * rows - flat.shape[0])).reshape(columns, rows)


def block(
    tokens,
    cotangent,
    lengths,
    ln1_gain,
    ln1_bias,
    qkv_weight,
    qkv_bias,
    out_weight,
    out_bias,
    ln2_gain,
    ln2_bias,
    up_weight,
    up_bias,
    down_weight,
    down_bias,
):
    dp = lax.axis_size(DP)
    _, model_width = tokens.shape
    shard_rows = model_width // dp
    head_local = qkv_bias.shape[1]
    head_width = qkv_bias.shape[2] * dp
    local_width = head_local * head_width
    pairs = head_local // 2
    hidden = up_weight.shape[1]

    vectors = jnp.stack([ln1_gain, ln1_bias, out_bias, ln2_gain, ln2_bias, down_bias])
    qkv_cols = as_columns(qkv_bias, shard_rows)
    up_cols = as_columns(up_bias, shard_rows)
    small = jnp.concatenate([vectors, qkv_cols, up_cols])
    small_width = -(-small.shape[0] // 128) * 128
    small = jnp.pad(small, ((0, small_width - small.shape[0]), (0, 0))).T
    parts = 2 if pairs % 2 == 0 else 1
    part_cols = 3 * local_width // parts
    qkv_shard = (
        qkv_weight.reshape(shard_rows, 3, pairs, 2 * head_width)
        .transpose(0, 2, 1, 3)
        .reshape(shard_rows, parts, part_cols)
    )
    columns = [[qkv_shard[:, part]] for part in range(parts)]
    columns[0].append(small)
    columns[-1].append(out_weight.T)
    shard_list = [jnp.concatenate(piece, axis=1) for piece in columns]
    up_shard, down_shard = up_weight, down_weight.T

    tokens_rest = gather_tensor(tokens)
    lines = [gather_line(shard_list[0])]
    for piece in shard_list[1:]:
        piece, *_ = tie(piece, *lines[-1])
        lines.append(gather_line(piece))
    cotangent_late, tokens_rest = tie(cotangent, tokens_rest)
    cotangent_rest = gather_tensor(cotangent_late)

    rest = [gather_rest(lines[0])]
    small_full = rest[0][:, part_cols : part_cols + small_width]

    wide = small_full.astype(jnp.float32).T
    norm1_gain, norm1_offset, out_shift, norm2_gain, norm2_offset, down_shift = (
        wide[i] for i in range(6)
    )
    qkv_at, up_at = 6, 6 + qkv_cols.shape[0]
    up_end = up_at + up_cols.shape[0]

    def from_columns(columns, like):
        count = columns.shape[0]
        blocks = columns.reshape(count, dp, shard_rows).transpose(1, 0, 2).reshape(dp, -1)
        return blocks[:, : like.size].reshape((dp,) + like.shape)

    qkv_bias_full = from_columns(wide[qkv_at:up_at], qkv_bias)
    qkv_bias_full = qkv_bias_full.transpose(1, 2, 0, 3).reshape(2, pairs, 2 * head_width)
    bias_parts = jnp.stack(
        [qkv_bias_full[0], jnp.zeros_like(qkv_bias_full[0]), qkv_bias_full[1]], axis=1
    ).reshape(parts, part_cols)
    up_shift = from_columns(wide[up_at:up_end], up_bias).transpose(1, 0, 2).reshape(hidden)

    token_float = tokens.astype(jnp.float32)
    scaled1, inverse1, pre_own = normalize(token_float, norm1_gain, norm1_offset)
    scaled1_rest, _, pre_rest = normalize(
        tokens_rest.astype(jnp.float32), norm1_gain, norm1_offset
    )
    normed1 = jnp.concatenate(
        relative(jnp.concatenate([pre_own.astype(jnp.bfloat16), pre_rest.astype(jnp.bfloat16)]))
    )

    def project(piece, bias):
        weight = piece[:, :part_cols]
        values = jnp.dot(normed1, weight, preferred_element_type=jnp.float32) + bias
        return weight, values.astype(jnp.bfloat16)

    up_piece, down_piece = up_shard, down_shard
    weight, part = project(rest[0], bias_parts[0])
    up_piece, *_ = tie(up_piece, *lines[-1])
    up_line = gather_line(up_piece)
    qkv_parts, projected = [weight], [part]
    for line, bias in zip(lines[1:], bias_parts[1:]):
        rest.append(gather_rest(line))
        weight, part = project(rest[-1], bias)
        qkv_parts.append(weight)
        projected.append(part)
    out_t = rest[-1][:, -local_width:]
    down_piece, *_ = tie(down_piece, *up_line)
    projected[-1], cotangent_rest = tie(projected[-1], cotangent_rest)
    down_line = gather_line(down_piece)
    attended = []
    for part in projected:
        attended.append(attention(lengths, part, head_width))
    mixed = jnp.concatenate([part[0] for part in attended], axis=1)
    mixed_own, *mixed_rest = relative(mixed)
    mixed_rest = jnp.concatenate(mixed_rest)
    up_full = gather_rest(up_line)
    out_rest = contract_cols(mixed_rest, out_t).astype(jnp.bfloat16)
    (out_own,) = tie(contract_cols(mixed_own, out_t))
    attended_out = scatter_tensor(out_own, out_rest)
    down_t = gather_rest(down_line)
    middle = token_float + attended_out + out_shift

    scaled2, inverse2, pre_two = normalize(middle, norm2_gain, norm2_offset)
    normed2_own = pre_two.astype(jnp.bfloat16)
    normed2_rest = gather_tensor(normed2_own)

    def feed_forward(normed, upstream):
        pre = jnp.dot(normed, up_full, preferred_element_type=jnp.float32) + up_shift
        grad_pre = jnp.dot(upstream, down_t, preferred_element_type=jnp.float32) * gelu_slope(pre)
        low = grad_pre.astype(jnp.bfloat16)
        return gelu_value(pre).astype(jnp.bfloat16), low, jnp.sum(grad_pre, axis=0)

    act_own, pre_own, up_sum_own = tie(*feed_forward(normed2_own, cotangent))
    act_rest, pre_rest, up_sum_rest = tie(*feed_forward(normed2_rest, cotangent_rest))
    grad_up_bias = up_sum_own + up_sum_rest
    norm_rest = contract_cols(pre_rest, up_full).astype(jnp.bfloat16)
    (norm_own,) = tie(contract_cols(pre_own, up_full))
    grad_norm2 = scatter_tensor(norm_own, norm_rest)
    activated = jnp.concatenate([act_own, act_rest])
    grad_pre_low = jnp.concatenate([pre_own, pre_rest])
    cotangent_all = jnp.concatenate([cotangent, cotangent_rest])
    normed2 = jnp.concatenate([normed2_own, normed2_rest])
    grad_down = contract_rows(cotangent_all, activated).astype(jnp.bfloat16)
    grad_up = contract_rows(normed2, grad_pre_low).astype(jnp.bfloat16)
    down_core = scatter_core([grad_down])
    up_core = scatter_core([grad_up])
    grad_down_bias = jnp.sum(cotangent.astype(jnp.float32), axis=0)
    grad_middle = cotangent.astype(jnp.float32) + normalize_back(
        grad_norm2, scaled2, inverse2, norm2_gain
    )
    seen = tie(grad_norm2, scaled2, grad_middle)
    grad_ln2_gain = jnp.sum(seen[0] * seen[1], axis=0)
    grad_ln2_bias = jnp.sum(seen[0], axis=0)
    grad_out_bias = jnp.sum(seen[2], axis=0)
    grad_middle_own = grad_middle.astype(jnp.bfloat16)
    grad_middle_rest = gather_tensor(grad_middle_own)
    down_side = scatter_side(*down_core)
    result_rest = contract_cols(act_rest, down_t).astype(jnp.bfloat16)
    (result_own,) = tie(contract_cols(act_own, down_t))
    feed = scatter_tensor(result_own, result_rest)
    feed, middle_late = tie(feed, middle)
    output = middle_late + feed + down_shift

    grad_middle_all = jnp.concatenate([grad_middle_own, grad_middle_rest])
    grad_mixed = jnp.dot(grad_middle_all, out_t, preferred_element_type=jnp.float32)
    grad_mixed = jnp.concatenate(relative(grad_mixed.astype(jnp.bfloat16)))
    up_side = scatter_side(*up_core)
    width = local_width // parts
    grad_parts, bias_parts = [], []
    down_own = scatter_line(*down_side)
    up_own = scatter_line(*up_side)
    for part in range(parts):
        upstream = grad_mixed[:, part * width : (part + 1) * width]
        grads, bias_sums = attention_back(
            lengths, projected[part], attended[part][0], upstream, attended[part][1], head_width
        )
        grad_parts.append(grads)
        bias_parts.append(bias_sums[:2])
    bias_sums = jnp.concatenate(bias_parts, axis=1)
    grad_out_t = contract_rows(
        grad_middle_all, jnp.concatenate([mixed_own, mixed_rest])
    ).astype(jnp.bfloat16)

    def first_grad(blocks):
        return sum(contract_cols(grads, weight) for grads, weight in zip(blocks, qkv_parts))

    by_owner = [relative(grads) for grads in grad_parts]
    part_rest = first_grad([jnp.concatenate(blocks[1:]) for blocks in by_owner])
    (part_own,) = tie(first_grad([blocks[0] for blocks in by_owner]))
    grad_norm1 = scatter_tensor(part_own, part_rest)
    seen_own, seen_rest, seen_scaled = tie(part_own, part_rest, scaled1)
    grad_ln1_gain, grad_ln1_bias = tie(
        jnp.sum(seen_own * seen_scaled, axis=0) + jnp.sum(seen_rest * scaled1_rest, axis=0),
        jnp.sum(seen_own, axis=0) + jnp.sum(seen_rest, axis=0),
    )
    grad_qkv = []
    for part, grads in enumerate(grad_parts):
        grad_qkv.append(contract_rows(normed1, grads).astype(jnp.bfloat16))

    def to_columns(values, count):
        padded = jnp.pad(values, ((0, 0), (0, count * shard_rows - values.shape[1])))
        return padded.reshape(dp, count, shard_rows).transpose(1, 0, 2).reshape(count, model_width)

    qkv_grads = bias_sums.reshape(2, head_local, dp, -1).transpose(2, 0, 1, 3).reshape(dp, -1)
    up_grads = grad_up_bias.reshape(up_bias.shape[0], dp, -1).transpose(1, 0, 2).reshape(dp, -1)
    sums = jnp.concatenate(
        [
            jnp.stack(
                [
                    grad_ln1_gain,
                    grad_ln1_bias,
                    grad_out_bias,
                    grad_ln2_gain,
                    grad_ln2_bias,
                    grad_down_bias,
                ]
            ),
            to_columns(qkv_grads, up_at - qkv_at),
            to_columns(up_grads, up_end - up_at),
        ]
    ).astype(jnp.bfloat16)
    sums = jnp.pad(sums, ((0, small_width - sums.shape[0]), (0, 0))).T
    pieces = [[part] for part in grad_qkv]
    pieces[0].append(grad_out_t)
    pieces[-1].append(sums)
    own = []
    for piece in pieces:
        core = scatter_core(piece)
        own.append(total_of(scatter_line(*scatter_side(*core))))
    up_shard, down_shard = total_of(up_own), total_of(down_own)
    down_final = down_shard.T
    out_shard = own[0][:, part_cols : part_cols + local_width]
    sums_own = own[-1][:, -small_width:].T[:up_end]
    qkv_shard = (
        jnp.concatenate([piece[:, :part_cols] for piece in own], axis=1)
        .reshape(shard_rows, pairs, 3, 2 * head_width)
        .transpose(0, 2, 1, 3)
        .reshape(shard_rows, 3, local_width)
    )
    vector_sums = sum_over(sums_own[:6], TP)
    grad_tokens = grad_middle + normalize_back(grad_norm1, scaled1, inverse1, norm1_gain)
    return (
        output,
        grad_tokens,
        vector_sums[0],
        vector_sums[1],
        qkv_shard,
        sums_own[qkv_at:up_at].reshape(-1)[: qkv_bias.size].reshape(qkv_bias.shape),
        out_shard.T,
        vector_sums[2],
        vector_sums[3],
        vector_sums[4],
        up_shard,
        sums_own[up_at:up_end].reshape(-1)[: up_bias.size].reshape(up_bias.shape),
        down_final,
        vector_sums[5],
    )


def solution(mesh):
    in_specs = (
        P((DP, TP), None),
        P((DP, TP), None),
        P(DP, None),
        P(DP),
        P(DP),
        P(DP, None, TP),
        P(None, TP, DP),
        P(TP, DP),
        P(DP),
        P(DP),
        P(DP),
        P(DP, TP),
        P(TP, DP),
        P(TP, DP),
        P(DP),
    )
    out_specs = (
        P((DP, TP), None),
        P((DP, TP), None),
        P(DP),
        P(DP),
        P(DP, None, TP),
        P(None, TP, DP),
        P(TP, DP),
        P(DP),
        P(DP),
        P(DP),
        P(DP, TP),
        P(TP, DP),
        P(TP, DP),
        P(DP),
    )
    return jax.shard_map(block, mesh=mesh, in_specs=in_specs, out_specs=out_specs, check_vma=False)
```

```python
import functools
import math

import jax
import jax.numpy as jnp
from jax import lax
from jax.experimental import pallas as pl
from jax.experimental.pallas import tpu as pltpu
from jax.sharding import PartitionSpec as P

epsilon = 1e-05
gelu_root = math.sqrt(2.0 / math.pi)
gelu_cubic = 0.044715
masked_score = -1e30


def normalize(values, norm_gain, offset):
    center = values - jnp.mean(values, axis=-1, keepdims=True)
    inverse = lax.rsqrt(jnp.mean(center * center, axis=-1, keepdims=True) + epsilon)
    scaled = center * inverse
    return (scaled, inverse, scaled * norm_gain + offset)


def normalize_back(upstream, scaled, inverse, norm_gain):
    weighted = upstream * norm_gain
    return inverse * (
        weighted
        - jnp.mean(weighted, axis=-1, keepdims=True)
        - scaled * jnp.mean(weighted * scaled, axis=-1, keepdims=True)
    )


def gelu_value(values):
    return (
        0.5
        * values
        * (1.0 + jnp.tanh(gelu_root * (values + gelu_cubic * values * values * values)))
    )


def gelu_slope(values):
    tangent = jnp.tanh(gelu_root * (values + gelu_cubic * values * values * values))
    inner_slope = gelu_root * (1.0 + 3.0 * gelu_cubic * values * values)
    return 0.5 * (1.0 + tangent) + 0.5 * values * (1.0 - tangent * tangent) * inner_slope


def contract_rows(left_rows, right_rows):
    return lax.dot_general(
        left_rows, right_rows, (((0,), (0,)), ((), ())), preferred_element_type=jnp.float32
    )


def contract_cols(left_rows, right_rows):
    return lax.dot_general(
        left_rows, right_rows, (((1,), (1,)), ((), ())), preferred_element_type=jnp.float32
    )


def lane_pair(rows, width):
    lane = lax.broadcasted_iota(jnp.int32, rows.shape, 1)
    zero = jnp.zeros_like(rows)
    first = jnp.where(lane < width, rows, zero)
    second = jnp.where(lane < width, zero, rows)
    return jnp.concatenate([first, second], axis=0)


def nt(left, right):
    return lax.dot_general(
        left, right, (((1,), (1,)), ((), ())), preferred_element_type=jnp.float32
    )


def nn(left, right):
    return lax.dot_general(
        left, right, (((1,), (0,)), ((), ())), preferred_element_type=jnp.float32
    )


def tile_pairs(group_rows, block, longest):
    count = group_rows // block
    first = [max(0, (i * block - longest + 1) // block) for i in range(count)]
    return [[j for j in range(first[i], i + 1)] for i in range(count)]


def fill_masks(lengths_ref, mask_ref, tiles, block):
    at = 0
    for i, keys in enumerate(tiles):
        query = i * block + lax.broadcasted_iota(jnp.int32, (1, block), 1)
        start = jnp.zeros((1, block), jnp.int32)
        end = jnp.int32(0)
        for s in range(lengths_ref.shape[1] - 1):
            end = end + lengths_ref[0, s]
            start = jnp.where(query >= end, end, start)
        for j in keys:
            key = j * block + lax.broadcasted_iota(jnp.int32, (block, block), 0)
            allowed = (key >= start) & (key <= query)
            mask_ref[at] = jnp.where(allowed, 0.0, masked_score).astype(jnp.float32)
            at += 1


def unpair(both, block, width):
    own = jnp.concatenate([both[:width, :block], both[width:, block:]], axis=0)
    return own.T


def attention_kernel(lengths_ref, x_ref, o_ref, lse_ref, mask_ref, vt_ref, *, tiles, block, width, scale):
    @pl.when(pl.program_id(0) == 0)
    def _():
        fill_masks(lengths_ref, mask_ref, tiles, block)

    pair = 2 * width
    vt_ref[...] = x_ref[:, 2 * pair : 3 * pair].T
    lse_ref[...] = jnp.zeros_like(lse_ref)
    at = 0
    for i, keys in enumerate(tiles):
        rows = slice(i * block, (i + 1) * block)
        queries = lane_pair(x_ref[rows, :pair], width)
        parts = []
        for t, j in enumerate(keys):
            score = nt(x_ref[j * block : (j + 1) * block, pair : 2 * pair], queries) * scale
            mask = mask_ref[at + t]
            parts.append(score + jnp.concatenate([mask, mask], axis=1))
        at += len(keys)
        peak = parts[0].max(axis=0, keepdims=True)
        for part in parts[1:]:
            peak = jnp.maximum(peak, part.max(axis=0, keepdims=True))
        total = jnp.zeros_like(peak)
        mixed = jnp.zeros((pair, 2 * block), jnp.float32)
        for part, j in zip(parts, keys):
            weight = jnp.exp(part - peak)
            total = total + weight.sum(axis=0, keepdims=True)
            mixed = mixed + nn(vt_ref[:, j * block : (j + 1) * block], weight.astype(jnp.bfloat16))
        o_ref[rows, :] = unpair(mixed / total, block, width).astype(o_ref.dtype)
        log_sum = peak + jnp.log(total)
        lse_ref[0:1, rows] = log_sum[:, :block]
        lse_ref[1:2, rows] = log_sum[:, block:]


def attention_back_kernel(
    lengths_ref, x_ref, o_ref, do_ref, lse_ref, g_ref, sum_ref, mask_ref, kt_ref, dk_ref, dv_ref, *, tiles, block, width, scale
):
    @pl.when(pl.program_id(0) == 0)
    def _():
        fill_masks(lengths_ref, mask_ref, tiles, block)

    pair = 2 * width
    kt_ref[...] = x_ref[:, pair : 2 * pair].T
    dk_ref[...] = jnp.zeros_like(dk_ref)
    dv_ref[...] = jnp.zeros_like(dv_ref)
    query_sum = jnp.zeros((1, pair), jnp.float32)
    at = 0
    for i, keys in enumerate(tiles):
        rows = slice(i * block, (i + 1) * block)
        queries = lane_pair(x_ref[rows, :pair], width)
        upstream = do_ref[rows, :]
        product = (upstream.astype(jnp.float32) * o_ref[rows, :].astype(jnp.float32)).T
        delta = jnp.concatenate(
            [
                product[:width].sum(axis=0, keepdims=True),
                product[width:].sum(axis=0, keepdims=True),
            ],
            axis=1,
        )
        log_sum = jnp.concatenate([lse_ref[0:1, rows], lse_ref[1:2, rows]], axis=1)
        upstream = lane_pair(upstream, width)
        grad_query = jnp.zeros((pair, 2 * block), jnp.float32)
        for j in keys:
            at_keys = slice(j * block, (j + 1) * block)
            score = nt(x_ref[at_keys, pair : 2 * pair], queries) * scale
            mask = mask_ref[at]
            at += 1
            weight = jnp.exp(score + jnp.concatenate([mask, mask], axis=1) - log_sum)
            grad_weight = nt(x_ref[at_keys, 2 * pair : 3 * pair], upstream)
            grad_score = (weight * (grad_weight - delta)).astype(jnp.bfloat16)
            dv_ref[at_keys, :] += nn(weight.astype(jnp.bfloat16), upstream)
            dk_ref[at_keys, :] += nn(grad_score, queries)
            grad_query = grad_query + nn(kt_ref[:, at_keys], grad_score)
        own = unpair(grad_query, block, width) * scale
        query_sum = query_sum + own.sum(axis=0, keepdims=True)
        g_ref[rows, :pair] = own.astype(g_ref.dtype)
    g_ref[:, pair : 2 * pair] = (dk_ref[...] * scale).astype(g_ref.dtype)
    g_ref[:, 2 * pair :] = dv_ref[...].astype(g_ref.dtype)
    sum_ref[...] = jnp.concatenate(
        [query_sum, dv_ref[...].sum(axis=0, keepdims=True), jnp.zeros((6, pair), jnp.float32)], axis=0
    )


def attention(lengths, projected, width):
    group_rows, columns = projected.shape
    pair = 2 * width
    count = columns // (3 * pair)
    block = min(256, group_rows)
    tiles = tile_pairs(group_rows, block, group_rows // 2)
    total = sum(len(keys) for keys in tiles)
    return pl.pallas_call(
        functools.partial(attention_kernel, tiles=tiles, block=block, width=width, scale=width**-0.5),
        out_shape=(
            jax.ShapeDtypeStruct((group_rows, count * pair), jnp.bfloat16),
            jax.ShapeDtypeStruct((count * 8, group_rows), jnp.float32),
        ),
        grid=(count,),
        in_specs=[
            pl.BlockSpec(memory_space=pltpu.SMEM),
            pl.BlockSpec((group_rows, 3 * pair), lambda p: (0, p)),
        ],
        out_specs=(
            pl.BlockSpec((group_rows, pair), lambda p: (0, p)),
            pl.BlockSpec((8, group_rows), lambda p: (p, 0)),
        ),
        scratch_shapes=[
            pltpu.VMEM((total, block, block), jnp.float32),
            pltpu.VMEM((pair, group_rows), jnp.bfloat16),
        ],
        compiler_params=pltpu.CompilerParams(vmem_limit_bytes=56 << 20),
        name="attention",
    )(lengths, projected)


def attention_back(lengths, projected, mixed, grad_mixed, log_sums, width):
    group_rows, columns = projected.shape
    pair = 2 * width
    count = columns // (3 * pair)
    block = min(256, group_rows)
    tiles = tile_pairs(group_rows, block, group_rows // 2)
    total = sum(len(keys) for keys in tiles)
    return pl.pallas_call(
        functools.partial(
            attention_back_kernel, tiles=tiles, block=block, width=width, scale=width**-0.5
        ),
        out_shape=(
            jax.ShapeDtypeStruct((group_rows, columns), jnp.bfloat16),
            jax.ShapeDtypeStruct((8, count * pair), jnp.float32),
        ),
        grid=(count,),
        in_specs=[
            pl.BlockSpec(memory_space=pltpu.SMEM),
            pl.BlockSpec((group_rows, 3 * pair), lambda p: (0, p)),
            pl.BlockSpec((group_rows, pair), lambda p: (0, p)),
            pl.BlockSpec((group_rows, pair), lambda p: (0, p)),
            pl.BlockSpec((8, group_rows), lambda p: (p, 0)),
        ],
        out_specs=(
            pl.BlockSpec((group_rows, 3 * pair), lambda p: (0, p)),
            pl.BlockSpec((8, pair), lambda p: (0, p)),
        ),
        scratch_shapes=[
            pltpu.VMEM((total, block, block), jnp.float32),
            pltpu.VMEM((pair, group_rows), jnp.bfloat16),
            pltpu.VMEM((group_rows, pair), jnp.float32),
            pltpu.VMEM((group_rows, pair), jnp.float32),
        ],
        compiler_params=pltpu.CompilerParams(vmem_limit_bytes=56 << 20),
        name="attention_back",
    )(lengths, projected, mixed, grad_mixed, log_sums)


DP, TP = "dp", "tensor"


def tie(*values):
    return lax.optimization_barrier(values)


def flip(value, axis_name, bit):
    size = lax.axis_size(axis_name)
    return lax.ppermute(value, axis_name, [(i, i ^ (1 << bit)) for i in range(size)])


def shift(value, axis_name, step, amount):
    size = lax.axis_size(axis_name)
    return lax.ppermute(value, axis_name, [(i, (i + amount * step) % size) for i in range(size)])


def place_kernel(where_ref, *refs):
    pieces, out_ref, sems = refs[:-2], refs[-2], refs[-1]
    line = pieces[0].shape[0]
    copies = []
    for p, piece in enumerate(pieces):
        for k in range(line):
            at = where_ref[p * line + k]
            copies.append(
                pltpu.make_async_copy(piece.at[k], out_ref.at[at], sems.at[p * line + k])
            )
    for copy in copies:
        copy.start()
    for copy in copies:
        copy.wait()


def place_blocks(pieces, where):
    line, rows, columns = pieces[0].shape
    blocks = line * len(pieces)
    out = pl.pallas_call(
        place_kernel,
        out_shape=jax.ShapeDtypeStruct((blocks, rows, columns), pieces[0].dtype),
        in_specs=[pl.BlockSpec(memory_space=pltpu.SMEM)]
        + [pl.BlockSpec(memory_space=pl.ANY)] * len(pieces),
        out_specs=pl.BlockSpec(memory_space=pltpu.VMEM),
        scratch_shapes=[pltpu.SemaphoreType.DMA((blocks,))],
        name="place_blocks",
    )
    out = out(where, *pieces)
    return out.reshape(blocks * rows, columns)


def gather_line(block):
    line = lax.axis_size(DP) // 4
    return [block] + [shift(block, DP, 4, k) for k in range(1, line)]


def gather_rest(blocks):
    line = len(blocks)
    own = jnp.stack(blocks)
    side = flip(own, DP, 1)
    index = lax.axis_index(DP)
    pieces = [own, side] + [flip(half, DP, 0) for half in (own, side)]
    back = (index // 4 - jnp.arange(line)) % line
    where = jnp.concatenate([back * 4 + ((index % 4) ^ mask) for mask in (0, 2, 1, 3)])
    return place_blocks(pieces, where.astype(jnp.int32))


def pick(values, at, axis):
    return lax.dynamic_index_in_dim(values, at, axis, keepdims=False)


def scatter_core(wholes):
    size = lax.axis_size(DP)
    core, *wholes = tie(lax.axis_index(DP) % 2, *wholes)
    blocks = [
        whole.reshape(size // 4, 2, 2, whole.shape[0] // size, whole.shape[1]) for whole in wholes
    ]

    def taken(at):
        return jnp.concatenate([pick(block, at, 2) for block in blocks], axis=-1)

    return taken(core), flip(taken(1 - core), DP, 0)


def scatter_side(kept, met):
    side = (lax.axis_index(DP) // 2) % 2

    def summed(at):
        return pick(kept, at, 1).astype(jnp.float32) + pick(met, at, 1).astype(jnp.float32)

    sent = summed(1 - side).astype(jnp.bfloat16)
    return summed(side), flip(sent, DP, 1)


def scatter_line(mine, crossed):
    line = mine.shape[0]
    at = lax.axis_index(DP) // 4
    sums = mine + crossed.astype(jnp.float32)
    low = sums.astype(jnp.bfloat16)
    return [pick(sums, at, 0)] + [
        shift(pick(low, (at + k) % line, 0), DP, 4, k) for k in range(1, line)
    ]


def total_of(parts):
    return sum(part.astype(jnp.float32) for part in parts)


def bits_of(size):
    count = size.bit_length() - 1
    assert size == 1 << count
    return count


def relative(whole):
    size = lax.axis_size(TP)
    blocks = whole.reshape((size, whole.shape[0] // size) + whole.shape[1:])
    return [pick(blocks, lax.axis_index(TP) ^ j, 0) for j in range(size)]


def gather_tensor(block):
    current = block
    for bit in range(bits_of(lax.axis_size(TP))):
        current = jnp.concatenate([current, flip(current, TP, bit)])
    return current[block.shape[0] :]


def scatter_tensor(own, rest):
    rows = own.shape[0]
    blocks = [own] + [rest[at : at + rows] for at in range(0, rest.shape[0], rows)]
    for bit in reversed(range(bits_of(lax.axis_size(TP)))):
        half = len(blocks) // 2
        sent = blocks[half:]
        sent = sent[0] if half == 1 else jnp.concatenate(sent)
        met = flip(sent.astype(jnp.bfloat16), TP, bit)
        blocks = [
            block + met[j * rows : (j + 1) * rows].astype(jnp.float32)
            for j, block in enumerate(blocks[:half])
        ]
    return blocks[0]


def sum_over(value, axis_name):
    for bit in range(bits_of(lax.axis_size(axis_name))):
        value = value + flip(value, axis_name, bit)
    return value


def as_columns(values, rows):
    flat = values.reshape(-1)
    columns = -(-flat.shape[0] // rows)
    return jnp.pad(flat, (0, columns * rows - flat.shape[0])).reshape(columns, rows)


def block(
    tokens,
    cotangent,
    lengths,
    ln1_gain,
    ln1_bias,
    qkv_weight,
    qkv_bias,
    out_weight,
    out_bias,
    ln2_gain,
    ln2_bias,
    up_weight,
    up_bias,
    down_weight,
    down_bias,
):
    dp = lax.axis_size(DP)
    _, model_width = tokens.shape
    shard_rows = model_width // dp
    head_local = qkv_bias.shape[1]
    head_width = qkv_bias.shape[2] * dp
    local_width = head_local * head_width
    pairs = head_local // 2
    hidden = up_weight.shape[1]

    vectors = jnp.stack([ln1_gain, ln1_bias, out_bias, ln2_gain, ln2_bias, down_bias])
    qkv_cols = as_columns(qkv_bias, shard_rows)
    up_cols = as_columns(up_bias, shard_rows)
    small = jnp.concatenate([vectors, qkv_cols, up_cols])
    small_width = -(-small.shape[0] // 128) * 128
    small = jnp.pad(small, ((0, small_width - small.shape[0]), (0, 0))).T
    parts = 2 if pairs % 2 == 0 else 1
    part_cols = 3 * local_width // parts
    qkv_shard = (
        qkv_weight.reshape(shard_rows, 3, pairs, 2 * head_width)
        .transpose(0, 2, 1, 3)
        .reshape(shard_rows, parts, part_cols)
    )
    columns = [[qkv_shard[:, part]] for part in range(parts)]
    columns[0].append(small)
    columns[-1].append(out_weight.T)
    shard_list = [jnp.concatenate(piece, axis=1) for piece in columns]
    up_shard, down_shard = up_weight, down_weight.T

    tokens_rest = gather_tensor(tokens)
    lines = [gather_line(shard_list[0])]
    for piece in shard_list[1:]:
        piece, *_ = tie(piece, *lines[-1])
        lines.append(gather_line(piece))
    cotangent_late, tokens_rest = tie(cotangent, tokens_rest)
    cotangent_rest = gather_tensor(cotangent_late)

    rest = [gather_rest(lines[0])]
    small_full = rest[0][:, part_cols : part_cols + small_width]

    wide = small_full.astype(jnp.float32).T
    norm1_gain, norm1_offset, out_shift, norm2_gain, norm2_offset, down_shift = (
        wide[i] for i in range(6)
    )
    qkv_at, up_at = 6, 6 + qkv_cols.shape[0]
    up_end = up_at + up_cols.shape[0]

    def from_columns(columns, like):
        count = columns.shape[0]
        blocks = columns.reshape(count, dp, shard_rows).transpose(1, 0, 2).reshape(dp, -1)
        return blocks[:, : like.size].reshape((dp,) + like.shape)

    qkv_bias_full = from_columns(wide[qkv_at:up_at], qkv_bias)
    qkv_bias_full = qkv_bias_full.transpose(1, 2, 0, 3).reshape(2, pairs, 2 * head_width)
    bias_parts = jnp.stack(
        [qkv_bias_full[0], jnp.zeros_like(qkv_bias_full[0]), qkv_bias_full[1]], axis=1
    ).reshape(parts, part_cols)
    up_shift = from_columns(wide[up_at:up_end], up_bias).transpose(1, 0, 2).reshape(hidden)

    token_float = tokens.astype(jnp.float32)
    scaled1, inverse1, pre_own = normalize(token_float, norm1_gain, norm1_offset)
    scaled1_rest, _, pre_rest = normalize(
        tokens_rest.astype(jnp.float32), norm1_gain, norm1_offset
    )
    scaled1, inverse1, scaled1_rest = tie(scaled1, inverse1, scaled1_rest)
    normed1 = jnp.concatenate(
        relative(jnp.concatenate([pre_own.astype(jnp.bfloat16), pre_rest.astype(jnp.bfloat16)]))
    )

    def project(piece, bias):
        weight = piece[:, :part_cols]
        values = jnp.dot(normed1, weight, preferred_element_type=jnp.float32) + bias
        return weight, values.astype(jnp.bfloat16)

    up_piece, down_piece = up_shard, down_shard
    weight, part = project(rest[0], bias_parts[0])
    up_piece, *_ = tie(up_piece, *lines[-1])
    up_line = gather_line(up_piece)
    qkv_parts, projected = [weight], [part]
    for line, bias in zip(lines[1:], bias_parts[1:]):
        rest.append(gather_rest(line))
        weight, part = project(rest[-1], bias)
        qkv_parts.append(weight)
        projected.append(part)
    out_t = rest[-1][:, -local_width:]
    down_piece, *_ = tie(down_piece, *up_line)
    projected[-1], cotangent_rest = tie(projected[-1], cotangent_rest)
    down_line = gather_line(down_piece)
    attended = []
    for part in projected:
        attended.append(attention(lengths, part, head_width))
    mixed = jnp.concatenate([part[0] for part in attended], axis=1)
    mixed_own, *mixed_rest = relative(mixed)
    mixed_rest = jnp.concatenate(mixed_rest)
    up_full = gather_rest(up_line)
    out_rest = contract_cols(mixed_rest, out_t).astype(jnp.bfloat16)
    (out_own,) = tie(contract_cols(mixed_own, out_t))
    attended_out = scatter_tensor(out_own, out_rest)
    down_t = gather_rest(down_line)
    middle = token_float + attended_out + out_shift

    scaled2, inverse2, pre_two = normalize(middle, norm2_gain, norm2_offset)
    normed2_own = pre_two.astype(jnp.bfloat16)
    normed2_rest = gather_tensor(normed2_own)

    def feed_forward(normed, upstream):
        pre = jnp.dot(normed, up_full, preferred_element_type=jnp.float32) + up_shift
        grad_pre = jnp.dot(upstream, down_t, preferred_element_type=jnp.float32) * gelu_slope(pre)
        low = grad_pre.astype(jnp.bfloat16)
        return gelu_value(pre).astype(jnp.bfloat16), low, jnp.sum(grad_pre, axis=0)

    act_own, pre_own, up_sum_own = tie(*feed_forward(normed2_own, cotangent))
    act_rest, pre_rest, up_sum_rest = tie(*feed_forward(normed2_rest, cotangent_rest))
    grad_up_bias = up_sum_own + up_sum_rest
    norm_rest = contract_cols(pre_rest, up_full).astype(jnp.bfloat16)
    (norm_own,) = tie(contract_cols(pre_own, up_full))
    grad_norm2 = scatter_tensor(norm_own, norm_rest)
    activated = jnp.concatenate([act_own, act_rest])
    grad_pre_low = jnp.concatenate([pre_own, pre_rest])
    cotangent_all = jnp.concatenate([cotangent, cotangent_rest])
    normed2 = jnp.concatenate([normed2_own, normed2_rest])
    grad_down = contract_rows(cotangent_all, activated).astype(jnp.bfloat16)
    grad_up = contract_rows(normed2, grad_pre_low).astype(jnp.bfloat16)
    down_core = scatter_core([grad_down])
    up_core = scatter_core([grad_up])
    grad_down_bias = jnp.sum(cotangent.astype(jnp.float32), axis=0)
    grad_middle = cotangent.astype(jnp.float32) + normalize_back(
        grad_norm2, scaled2, inverse2, norm2_gain
    )
    seen = tie(grad_norm2, scaled2, grad_middle)
    grad_ln2_gain = jnp.sum(seen[0] * seen[1], axis=0)
    grad_ln2_bias = jnp.sum(seen[0], axis=0)
    grad_out_bias = jnp.sum(seen[2], axis=0)
    grad_middle_own = grad_middle.astype(jnp.bfloat16)
    grad_middle_rest = gather_tensor(grad_middle_own)
    down_side = scatter_side(*down_core)
    result_rest = contract_cols(act_rest, down_t).astype(jnp.bfloat16)
    (result_own,) = tie(contract_cols(act_own, down_t))
    feed = scatter_tensor(result_own, result_rest)
    feed, middle_late = tie(feed, middle)
    output = middle_late + feed + down_shift

    grad_middle_all = jnp.concatenate([grad_middle_own, grad_middle_rest])
    grad_mixed = jnp.dot(grad_middle_all, out_t, preferred_element_type=jnp.float32)
    grad_mixed = jnp.concatenate(relative(grad_mixed.astype(jnp.bfloat16)))
    up_side = scatter_side(*up_core)
    width = local_width // parts
    grad_parts, bias_parts = [], []
    down_own = scatter_line(*down_side)
    up_own = scatter_line(*up_side)
    for part in range(parts):
        upstream = grad_mixed[:, part * width : (part + 1) * width]
        grads, bias_sums = attention_back(
            lengths, projected[part], attended[part][0], upstream, attended[part][1], head_width
        )
        grad_parts.append(grads)
        bias_parts.append(bias_sums[:2])
    bias_sums = jnp.concatenate(bias_parts, axis=1)
    grad_out_t = contract_rows(
        grad_middle_all, jnp.concatenate([mixed_own, mixed_rest])
    ).astype(jnp.bfloat16)

    def first_grad(blocks):
        return sum(contract_cols(grads, weight) for grads, weight in zip(blocks, qkv_parts))

    by_owner = [relative(grads) for grads in grad_parts]
    part_rest = first_grad([jnp.concatenate(blocks[1:]) for blocks in by_owner])
    (part_own,) = tie(first_grad([blocks[0] for blocks in by_owner]))
    grad_norm1 = scatter_tensor(part_own, part_rest)
    seen_own, seen_rest = tie(part_own, part_rest)
    grad_ln1_gain, grad_ln1_bias = tie(
        jnp.sum(seen_own * scaled1, axis=0) + jnp.sum(seen_rest * scaled1_rest, axis=0),
        jnp.sum(seen_own, axis=0) + jnp.sum(seen_rest, axis=0),
    )
    grad_qkv = []
    for part, grads in enumerate(grad_parts):
        grad_qkv.append(contract_rows(normed1, grads).astype(jnp.bfloat16))

    def to_columns(values, count):
        padded = jnp.pad(values, ((0, 0), (0, count * shard_rows - values.shape[1])))
        return padded.reshape(dp, count, shard_rows).transpose(1, 0, 2).reshape(count, model_width)

    qkv_grads = bias_sums.reshape(2, head_local, dp, -1).transpose(2, 0, 1, 3).reshape(dp, -1)
    up_grads = grad_up_bias.reshape(up_bias.shape[0], dp, -1).transpose(1, 0, 2).reshape(dp, -1)
    sums = jnp.concatenate(
        [
            jnp.stack(
                [
                    grad_ln1_gain,
                    grad_ln1_bias,
                    grad_out_bias,
                    grad_ln2_gain,
                    grad_ln2_bias,
                    grad_down_bias,
                ]
            ),
            to_columns(qkv_grads, up_at - qkv_at),
            to_columns(up_grads, up_end - up_at),
        ]
    ).astype(jnp.bfloat16)
    sums = jnp.pad(sums, ((0, small_width - sums.shape[0]), (0, 0))).T
    pieces = [[part] for part in grad_qkv]
    pieces[0].append(grad_out_t)
    pieces[-1].append(sums)
    own = []
    for piece in pieces:
        core = scatter_core(piece)
        own.append(total_of(scatter_line(*scatter_side(*core))))
    up_shard, down_shard = total_of(up_own), total_of(down_own)
    down_final = down_shard.T
    out_shard = own[0][:, part_cols : part_cols + local_width]
    sums_own = own[-1][:, -small_width:].T[:up_end]
    qkv_shard = (
        jnp.concatenate([piece[:, :part_cols] for piece in own], axis=1)
        .reshape(shard_rows, pairs, 3, 2 * head_width)
        .transpose(0, 2, 1, 3)
        .reshape(shard_rows, 3, local_width)
    )
    vector_sums = sum_over(sums_own[:6], TP)
    grad_tokens = grad_middle + normalize_back(grad_norm1, scaled1, inverse1, norm1_gain)
    return (
        output,
        grad_tokens,
        vector_sums[0],
        vector_sums[1],
        qkv_shard,
        sums_own[qkv_at:up_at].reshape(-1)[: qkv_bias.size].reshape(qkv_bias.shape),
        out_shard.T,
        vector_sums[2],
        vector_sums[3],
        vector_sums[4],
        up_shard,
        sums_own[up_at:up_end].reshape(-1)[: up_bias.size].reshape(up_bias.shape),
        down_final,
        vector_sums[5],
    )


def solution(mesh):
    in_specs = (
        P((DP, TP), None),
        P((DP, TP), None),
        P(DP, None),
        P(DP),
        P(DP),
        P(DP, None, TP),
        P(None, TP, DP),
        P(TP, DP),
        P(DP),
        P(DP),
        P(DP),
        P(DP, TP),
        P(TP, DP),
        P(TP, DP),
        P(DP),
    )
    out_specs = (
        P((DP, TP), None),
        P((DP, TP), None),
        P(DP),
        P(DP),
        P(DP, None, TP),
        P(None, TP, DP),
        P(TP, DP),
        P(DP),
        P(DP),
        P(DP),
        P(DP, TP),
        P(TP, DP),
        P(TP, DP),
        P(DP),
    )
    return jax.shard_map(block, mesh=mesh, in_specs=in_specs, out_specs=out_specs, check_vma=False)
```
